32 devices in a mesh: wide: 8 (over y, x, core), narrow: 4 (over z).
Axes of the slice: x: 2, y: 2, z: 4, core: 2. Of those that a mesh axis runs over, the one named last changes fastest.
Arguments:
- reference_image: bfloat16 [1024, 512, 128], P('wide', 'narrow'), may hold values from -6 to 6
- deformed_image: bfloat16 [1024, 512, 128], P('wide', 'narrow'), may hold values from -6 to 6
- displacement: float32 [3, 17, 128, 64], P(None, None, 'wide', 'narrow'), may hold values from -0.5 to 0.5
- tile_map: int32 [8, 4, 2], P('wide', 'narrow'), may hold values from -32 to 32, as said below
Outputs:
- updated: float32 [3, 17, 128, 64], P(None, None, 'wide', 'narrow')
- residual: bfloat16 [1024, 512, 128], P('wide', 'narrow')
The draws below stay inside these ranges and needn't reach their ends.
Inputs may be any that keep to these rules, and one draw needn't show every extreme that they name: `tile_map`: each component spans -32 to 32 over the tiles and reaches both ends on some tile.
All inputs are finite; a program needn't handle non-finite values.
Results may differ from the reference program's by a relative error of at most 0.0004.
Values may be sent and summed in bfloat16 or wider, within the bound.
A program may use at most 256 MiB of HBM per device.

```python
import jax
import jax.numpy as jnp
from jax import lax

TX = 128
TY = 128
Z = 128
RIM = 32
EX = 16
EY = 16
S = 17
NTX = 8
NTY = 4
NX = 1024
NY = 512
NXE = 128
NYE = 64


def draw_tile_map(key, part):
    first_key = jax.random.fold_in(key, 11)
    second_key = jax.random.fold_in(key, 12)
    offsets = jax.random.randint(first_key, (NTX * NTY, 2), -RIM, RIM + 1, dtype=jnp.int32)
    chosen = jax.random.permutation(second_key, NTX * NTY)[:4]
    offsets = offsets.at[chosen[0], 0].set(RIM)
    offsets = offsets.at[chosen[1], 0].set(-RIM)
    offsets = offsets.at[chosen[2], 1].set(RIM)
    offsets = offsets.at[chosen[3], 1].set(-RIM)
    return offsets.reshape(NTX, NTY, 2)


def block_levels(own_key, extent, cuts, smallest, largest):
    gain = 1.0
    for dim, blocks in cuts:
        steps = jax.random.uniform(jax.random.fold_in(jax.random.fold_in(own_key, 6), dim), (blocks,), jnp.float32, smallest / len(cuts), largest / len(cuts))
        gain = gain * jnp.repeat(jnp.exp(steps), extent[dim] // blocks).reshape((-1,) + (1,) * (len(extent) - 1 - dim))
    return gain


def gaussian(key, shape, deviation, reach, pieces=(), kind=jnp.bfloat16):
    drawn = deviation * jax.random.normal(key, shape, jnp.float32)
    if pieces:
        drawn = drawn * block_levels(key, shape, pieces, -0.22, 0.18)
    return jnp.clip(drawn, -reach, reach).astype(kind)


def setup_inputs(seed: int = 0) -> dict:
    arg_keys = jax.random.split(jax.random.key(seed), 5)
    reference_image = gaussian(arg_keys[0], (NX, NY, Z), 1.0, 6.0, ((0, 8), (1, 4)))
    deformed_image = gaussian(arg_keys[1], (NX, NY, Z), 1.0, 6.0, ((0, 8), (1, 4)))
    displacement = jnp.clip(jax.random.uniform(arg_keys[2], (3, S, NXE, NYE), jnp.float32, -0.5, 0.5) * block_levels(arg_keys[2], (3, S, NXE, NYE), ((2, 8), (3, 4)), -0.4, 0.0), -0.5, 0.5)
    tile_map = draw_tile_map(jax.random.fold_in(arg_keys[4], 71), 0)
    return dict(reference_image=reference_image, deformed_image=deformed_image, displacement=displacement, tile_map=tile_map)


MU_SHEAR = 1.0
LAMBDA_BULK = 2.0
REG_WEIGHT = 256.0
STIFFNESS = 16.0
PRECISE = lax.Precision.HIGHEST

def shape_table(voxels):
    cell_ids = jnp.arange(voxels, dtype=jnp.int32)
    element = cell_ids // 8
    fraction = ((cell_ids % 8).astype(jnp.float32) + 0.5) / 8.0
    node_ids = jnp.arange(voxels // 8 + 1, dtype=jnp.int32)
    lower_part = jnp.where(node_ids[None, :] == element[:, None], 1.0 - fraction[:, None], 0.0)
    upper_part = jnp.where(node_ids[None, :] == element[:, None] + 1, fraction[:, None], 0.0)
    return (lower_part + upper_part).astype(jnp.float32)

def interpolate(nodal_field, table_x, table_y, table_z):
    step_one = jnp.einsum('zs,cspq->czpq', table_z, nodal_field, precision=PRECISE)
    step_two = jnp.einsum('xp,czpq->cxzq', table_x, step_one, precision=PRECISE)
    return jnp.einsum('yq,cxzq->cxyz', table_y, step_two, precision=PRECISE)

def project(field, table_x, table_y, table_z):
    step_one = jnp.einsum('yq,cxyz->cxzq', table_y, field, precision=PRECISE)
    step_two = jnp.einsum('xp,cxzq->czpq', table_x, step_one, precision=PRECISE)
    return jnp.einsum('zs,czpq->cspq', table_z, step_two, precision=PRECISE)

def tile_terms(reference_tile, window, nodal_field):
    table_x = shape_table(reference_tile.shape[0])
    table_y = shape_table(reference_tile.shape[1])
    table_z = shape_table(reference_tile.shape[2])
    sampled = window[1:-1, 1:-1, :]
    slope_x = 0.5 * (window[2:, 1:-1, :] - window[:-2, 1:-1, :])
    slope_y = 0.5 * (window[1:-1, 2:, :] - window[1:-1, :-2, :])
    padded_z = jnp.pad(sampled, ((0, 0), (0, 0), (1, 1)))
    slope_z = 0.5 * (padded_z[:, :, 2:] - padded_z[:, :, :-2])
    moved = interpolate(nodal_field, table_x, table_y, table_z)
    residual = reference_tile - sampled - (slope_x * moved[0] + slope_y * moved[1] + slope_z * moved[2])
    slopes = jnp.stack([slope_x, slope_y, slope_z])
    data_grad = -project(slopes * residual[None], table_x, table_y, table_z)
    data_diag = project(slopes * slopes, table_x * table_x, table_y * table_y, table_z * table_z)
    return (residual, data_grad, data_diag)

def element_energy(nodal_field):
    diff_x = nodal_field[:, :, 1:, :] - nodal_field[:, :, :-1, :]
    grad_x = 0.03125 * (diff_x[:, :-1, :, :-1] + diff_x[:, 1:, :, :-1] + diff_x[:, :-1, :, 1:] + diff_x[:, 1:, :, 1:])
    diff_y = nodal_field[:, :, :, 1:] - nodal_field[:, :, :, :-1]
    grad_y = 0.03125 * (diff_y[:, :-1, :-1, :] + diff_y[:, 1:, :-1, :] + diff_y[:, :-1, 1:, :] + diff_y[:, 1:, 1:, :])
    diff_z = nodal_field[:, 1:, :, :] - nodal_field[:, :-1, :, :]
    grad_z = 0.03125 * (diff_z[:, :, :-1, :-1] + diff_z[:, :, 1:, :-1] + diff_z[:, :, :-1, 1:] + diff_z[:, :, 1:, 1:])
    columns = (grad_x, grad_y, grad_z)
    entries = [[columns[j][i] + (1.0 if i == j else 0.0) for j in range(3)] for i in range(3)]
    volume_ratio = entries[0][0] * (entries[1][1] * entries[2][2] - entries[1][2] * entries[2][1]) - entries[0][1] * (entries[1][0] * entries[2][2] - entries[1][2] * entries[2][0]) + entries[0][2] * (entries[1][0] * entries[2][1] - entries[1][1] * entries[2][0])
    squares = entries[0][0] * entries[0][0]
    for i in range(3):
        for j in range(3):
            if i + j > 0:
                squares = squares + entries[i][j] * entries[i][j]
    log_ratio = jnp.log(volume_ratio)
    energy = 0.5 * MU_SHEAR * (squares - 3.0 - 2.0 * log_ratio) + 0.5 * LAMBDA_BULK * log_ratio * log_ratio
    return REG_WEIGHT * jnp.sum(energy)

def pad_nodes(nodal_field):
    return jnp.pad(nodal_field, ((0, 0), (0, 0), (0, 1), (0, 1)))

def reference(reference_image, deformed_image, displacement, tile_map):
    margin = RIM + 1
    deformed = jnp.pad(deformed_image.astype(jnp.float32), ((margin, margin), (margin, margin), (0, 0)))
    reference_full = reference_image.astype(jnp.float32)
    nodal_full = pad_nodes(displacement)

    def one_tile(number):
        tile_row = (number // NTY).astype(jnp.int32)
        tile_col = (number % NTY).astype(jnp.int32)
        offset_x = tile_map[tile_row, tile_col, 0]
        offset_y = tile_map[tile_row, tile_col, 1]
        window = lax.dynamic_slice(deformed, (tile_row * TX + offset_x + margin - 1, tile_col * TY + offset_y + margin - 1, jnp.int32(0)), (TX + 2, TY + 2, Z))
        reference_tile = lax.dynamic_slice(reference_full, (tile_row * TX, tile_col * TY, jnp.int32(0)), (TX, TY, Z))
        nodal_tile = lax.dynamic_slice(nodal_full, (jnp.int32(0), jnp.int32(0), tile_row * EX, tile_col * EY), (3, S, EX + 1, EY + 1))
        residual, data_grad, data_diag = tile_terms(reference_tile, window, nodal_tile)
        return (residual.astype(jnp.bfloat16), data_grad, data_diag)
    residuals, grads, diags = lax.map(one_tile, jnp.arange(NTX * NTY, dtype=jnp.int32))

    def add_tile(number, totals):
        number = jnp.asarray(number).astype(jnp.int32)
        tile_row = number // NTY
        tile_col = number % NTY
        corner = (jnp.int32(0), jnp.int32(0), tile_row * EX, tile_col * EY)
        grad_total = lax.dynamic_update_slice(totals[0], lax.dynamic_slice(totals[0], corner, (3, S, EX + 1, EY + 1)) + grads[number], corner)
        diag_total = lax.dynamic_update_slice(totals[1], lax.dynamic_slice(totals[1], corner, (3, S, EX + 1, EY + 1)) + diags[number], corner)
        return (grad_total, diag_total)
    blank = jnp.zeros((3, S, NXE + 1, NYE + 1), jnp.float32)
    grad_total, diag_total = lax.fori_loop(0, NTX * NTY, add_tile, (blank, blank))
    reg_grad = jax.grad(lambda nodal_field: element_energy(pad_nodes(nodal_field)))(displacement)
    gradient = grad_total[:, :, :NXE, :NYE] + reg_grad
    diagonal = diag_total[:, :, :NXE, :NYE] + STIFFNESS
    updated = displacement - gradient / diagonal
    residual = residuals.reshape(NTX, NTY, TX, TY, Z).transpose(0, 2, 1, 3, 4).reshape(NX, NY, Z)
    return (updated, residual)
```

```python
import functools

import jax
import jax.numpy as jnp
import numpy as np
from jax import lax
from jax.experimental import pallas as pl
from jax.experimental.pallas import tpu as pltpu
from jax.sharding import PartitionSpec as P

MU_SHEAR = 1.0
LAMBDA_BULK = 2.0
REG_WEIGHT = 256.0
STIFFNESS = 16.0
MESH = pl.DeviceIdType.MESH
F32 = jnp.float32
BF16 = jnp.bfloat16
SIDE = 48
QPAD = 24


def shifted(array, axis, by):
    size = lax.axis_size(axis)
    pairs = [(i, i + by) for i in range(size) if 0 <= i + by < size]
    return lax.ppermute(array, axis, pairs)


def halo_kernel(nw, nn, rim, own, ext, zeros, send, recv, zsem, lsem):
    rows, cols, _ = own.shape
    w = lax.axis_index("wide")
    n = lax.axis_index("narrow")
    lo_w, hi_w, lo_n, hi_n = w > 0, w < nw - 1, n > 0, n < nn - 1
    up_w, dn_w = (w + 1, n), (w - 1, n)
    up_n, dn_n = (w, n + 1), (w, n - 1)
    mid = slice(SIDE, SIDE + cols)
    ylo = slice(0, SIDE)
    yhi = slice(SIDE + cols, SIDE + cols + SIDE)
    barrier = pltpu.get_barrier_semaphore()
    sides = ((lo_w, dn_w), (hi_w, up_w), (lo_n, dn_n), (hi_n, up_n))
    for there, device in sides:
        @pl.when(there)
        def _(device=device):
            pl.semaphore_signal(barrier, inc=1, device_id=device, device_id_type=MESH)
    zeros[...] = jnp.zeros_like(zeros)
    as_int = lambda flag: flag.astype(jnp.int32)
    pl.semaphore_wait(barrier, as_int(lo_w) + as_int(hi_w) + as_int(lo_n) + as_int(hi_n))

    def remote(k, src, dst, device):
        return pltpu.make_async_remote_copy(
            src_ref=src, dst_ref=dst, send_sem=send.at[k], recv_sem=recv.at[k],
            device_id=device, device_id_type=MESH)

    full = (slice(0, rim), slice(rim, rows - rim), slice(rows - rim, rows))
    copies = []
    for j in (0, 2, 1):
        part = full[j]
        there = slice(part.start + rim, part.stop + rim)
        copies.append((hi_n, lo_n, remote(j, own.at[part, cols - SIDE:cols], ext.at[there, ylo], up_n)))
        copies.append((lo_n, hi_n, remote(3 + j, own.at[part, 0:SIDE], ext.at[there, yhi], dn_n)))
    copies.append((hi_w, lo_w, remote(6, own.at[rows - rim:rows], ext.at[0:rim, mid], up_w)))
    copies.append((lo_w, hi_w, remote(7, own.at[0:rim], ext.at[rows + rim:rows + 2 * rim, mid], dn_w)))
    for goes, _c, copy in copies:
        @pl.when(goes)
        def _(copy=copy):
            copy.start()
    local = pltpu.make_async_copy(own, ext.at[rim:rim + rows, mid], lsem)
    local.start()
    total = rows + 2 * rim

    def fills():
        out = []
        out.append((jnp.logical_not(lo_n), 0, zeros.at[:, 0:SIDE], ext.at[:, ylo]))
        out.append((jnp.logical_not(hi_n), 1, zeros.at[:, 0:SIDE], ext.at[:, yhi]))
        out.append((jnp.logical_not(lo_w), 2, None, slice(0, rim)))
        out.append((jnp.logical_not(hi_w), 3, None, slice(rim + rows, total)))
        return out

    jobs = []
    for cond, k, src, dst in fills()[:2]:
        jobs.append((cond, pltpu.make_async_copy(src, dst, zsem.at[k])))
    for k, (cond, band) in enumerate(((jnp.logical_not(lo_w), slice(0, rim)), (jnp.logical_not(hi_w), slice(rim + rows, total)))):
        jobs.append((cond, pltpu.make_async_copy(zeros.at[0:rim, 0:cols], ext.at[band, mid], zsem.at[2 + k])))
        jobs.append((cond & lo_n, pltpu.make_async_copy(zeros.at[0:rim, 0:SIDE], ext.at[band, ylo], zsem.at[4 + k])))
        jobs.append((cond & hi_n, pltpu.make_async_copy(zeros.at[0:rim, 0:SIDE], ext.at[band, yhi], zsem.at[6 + k])))
    for cond, job in jobs:
        @pl.when(cond)
        def _(job=job):
            job.start()
    corners = []
    low_rows, high_rows = slice(rim, 2 * rim), slice(rows, rows + rim)
    below, above = slice(0, rim), slice(rim + rows, total)
    corners.append((lo_n & lo_w, lo_n & hi_w, remote(8, ext.at[low_rows, ylo], ext.at[above, ylo], dn_w)))
    corners.append((hi_n & lo_w, hi_n & hi_w, remote(9, ext.at[low_rows, yhi], ext.at[above, yhi], dn_w)))
    corners.append((lo_n & hi_w, lo_n & lo_w, remote(10, ext.at[high_rows, ylo], ext.at[below, ylo], up_w)))
    corners.append((hi_n & hi_w, hi_n & lo_w, remote(11, ext.at[high_rows, yhi], ext.at[below, yhi], up_w)))
    for (_g, comes, copy), corner in zip(copies[:4], corners):
        @pl.when(comes)
        def _(copy=copy):
            copy.wait_recv()
        @pl.when(corner[0])
        def _(corner=corner):
            corner[2].start()
    for _g, comes, copy in copies[4:] + corners:
        @pl.when(comes)
        def _(copy=copy):
            copy.wait_recv()
    for goes, _c, copy in copies + corners:
        @pl.when(goes)
        def _(copy=copy):
            copy.wait_send()
    for cond, job in jobs:
        @pl.when(cond)
        def _(job=job):
            job.wait()
    local.wait()


def exchange(deformed, nw, nn):
    rows, cols, layers = deformed.shape
    rim = rows // 4 + 1
    shape = (rows + 2 * rim, cols + 2 * SIDE, layers)
    return pl.pallas_call(
        functools.partial(halo_kernel, nw, nn, rim),
        out_shape=jax.ShapeDtypeStruct(shape, BF16),
        in_specs=[pl.BlockSpec(memory_space=pl.ANY)],
        out_specs=pl.BlockSpec(memory_space=pl.ANY),
        scratch_shapes=[
            pltpu.VMEM((shape[0], cols, layers), BF16),
            pltpu.SemaphoreType.DMA((12,)),
            pltpu.SemaphoreType.DMA((12,)),
            pltpu.SemaphoreType.DMA((8,)),
            pltpu.SemaphoreType.DMA,
        ],
        compiler_params=pltpu.CompilerParams(
            collective_id=0, has_side_effects=True, vmem_limit_bytes=32 << 20),
        name="halo",
    )(deformed)


def tables(rows, cols, layers, comps):
    def one(voxels):
        t = np.zeros((voxels, voxels // 8 + 1))
        for i in range(voxels):
            f = (i % 8 + 0.5) / 8.0
            t[i, i // 8] += 1.0 - f
            t[i, i // 8 + 1] += f
        return t
    ty, tz = one(cols), one(layers)
    nq, ns = ty.shape[1], tz.shape[1]
    typ = np.zeros((cols, QPAD))
    typ[:, :nq] = ty
    frac = (np.arange(8) + 0.5) / 8.0
    wx = np.stack([1.0 - frac, frac], 1)
    inter = 0.5 * np.einsum("ka,yq->kyaq", wx, typ)
    inter = np.concatenate([inter[:, :, 0], inter[:, :, 0], inter[:, :, 1], inter[:, :, 1]], -1)
    inter = inter.reshape(8 * cols, 4 * QPAD)
    proj = np.concatenate([typ.T, typ.T], 1)
    diag = np.einsum("ka,yq->aqky", wx * wx, typ * typ).reshape(2 * QPAD, 8 * cols)
    dhi = diag.astype(BF16).astype(np.float64)
    diag = np.concatenate([dhi, diag - dhi], 0)
    lanes = comps * layers
    up = np.zeros((2 * comps * ns, lanes))
    down = np.zeros((lanes, 128))
    down2 = np.zeros((lanes, 128))
    for c in range(comps):
        for h in range(2):
            up[(h * comps + c) * ns:(h * comps + c + 1) * ns, c * layers:(c + 1) * layers] = tz.T
        down[c * layers:(c + 1) * layers, c * ns:(c + 1) * ns] = -0.5 * tz
        down2[c * layers:(c + 1) * layers, c * ns:(c + 1) * ns] = 0.25 * tz * tz
    dz = np.zeros((layers, layers))
    for z in range(layers):
        if z + 1 < layers:
            dz[z + 1, z] = 1.0
        if z > 0:
            dz[z - 1, z] = -1.0
    as_bf16 = lambda a: jnp.asarray(a.astype(BF16))
    return [as_bf16(a) for a in (inter, proj, diag, up, down, down2, dz)]


def split(value):
    high = value.astype(BF16)
    return high, (value - high.astype(F32)).astype(BF16)


def tile_kernel(rim, map_ref, ref_tile, ext, nodes, inter, proj, diag, up, down, down2, dz,
                res, grad_out, diag_out,
                rows_in, shift, samp, ndz, moved, gy, gz, sums, sq, gacc, dacc, sem):
    p = pl.program_id(0)
    steps = pl.num_programs(0)
    cols, layers = samp.shape[1], samp.shape[2]
    comps = ndz.shape[2] // layers
    start = map_ref[0] + (rim - 1)

    def fetch(first, count, k):
        return pltpu.make_async_copy(
            ext.at[pl.ds(start + first, count)], rows_in.at[pl.ds(first, count)], sem.at[k])

    def sample(first, count):
        for a in range(0, count, 2):
            pair = jnp.concatenate([rows_in[first + a], rows_in[first + a + 1]], axis=1)
            got = jnp.dot(shift[...], pair, preferred_element_type=F32)
            for b in range(2):
                samp[first + a + b] = got[:cols, b * layers:(b + 1) * layers]
                gy[(first + a + b) % 16] = got[cols:, b * layers:(b + 1) * layers]

    @pl.when(p == 0)
    def _():
        fetch(0, 2, steps).start()

        @pl.loop(0, steps)
        def _(k):
            fetch(8 * k + 2, 8, k).start()
        y = lax.broadcasted_iota(jnp.int32, (cols, shift.shape[1]), 0)
        k = lax.broadcasted_iota(jnp.int32, (cols, shift.shape[1]), 1)
        gap = k - y - (map_ref[1] + SIDE)
        shift[:cols] = jnp.where(gap == 0, 1.0, 0.0).astype(BF16)
        shift[cols:] = (jnp.where(gap == 1, 1.0, 0.0) - jnp.where(gap == -1, 1.0, 0.0)).astype(BF16)
        high = nodes[...].astype(BF16).astype(F32)
        both = jnp.concatenate([high, nodes[...] - high], axis=1).astype(BF16)
        level = jnp.dot(both, up[...], preferred_element_type=F32)
        for i in range(ndz.shape[0]):
            part = level[i * QPAD:(i + 1) * QPAD]
            head = part.astype(BF16).astype(F32)
            ndz[i] = jnp.concatenate([head, part - head], axis=0).astype(BF16)
        gacc[...] = jnp.zeros_like(gacc)
        dacc[...] = jnp.zeros_like(dacc)
        fetch(0, 2, steps).wait()
        sample(0, 2)

    base = pl.multiple_of(8 * p, 8)
    fetch(base + 2, 8, p).wait()
    sample(base + 2, 8)
    gz[...] = jnp.dot(samp[pl.ds(base + 1, 8)].reshape(8 * cols, layers).astype(BF16), dz[...],
                      preferred_element_type=F32)
    level = ndz[pl.ds(p, 2)].reshape(4 * QPAD, comps * layers)
    moved[...] = jnp.dot(inter[...], level, preferred_element_type=F32)

    chunk = 32

    @pl.loop(0, cols // chunk)
    def _(j):
        at = pl.multiple_of(j * chunk, chunk)
        span = pl.ds(at, chunk)
        run = [None] * comps
        tot = [None] * comps
        for k in range(8):
            line = pl.ds(k * cols + at, chunk)
            here = samp[base + 1 + k, span, :]
            g = [samp[base + 2 + k, span, :] - samp[base + k, span, :],
                 gy[(base + 1 + k) % 16, span, :],
                 gz[line, :]]
            r = ref_tile[k, span, :].astype(F32) - here
            for c in range(3):
                r = r - g[c] * moved[line, c * layers:(c + 1) * layers]
            res[k, span, :] = r.astype(BF16)
            for c in range(3):
                f = g[c] * r
                run[c] = f if k == 0 else run[c] + f
                tot[c] = run[c] if k == 0 else tot[c] + run[c]
                sq[line, c * layers:(c + 1) * layers] = (g[c] * g[c]).astype(BF16)
        for c in range(3):
            low = (tot[c] - 0.5 * run[c]) * 0.125
            for a, value in enumerate((low, run[c] - low)):
                head, tail = split(value)
                sums[a, span, c * layers:(c + 1) * layers] = head
                sums[a, pl.ds(cols + at, chunk), c * layers:(c + 1) * layers] = tail

    for a in range(2):
        gacc[p + a] = gacc[p + a] + jnp.dot(proj[...], sums[a], preferred_element_type=F32)
    got = jnp.dot(diag[...], sq[...], preferred_element_type=F32)
    for a in range(2):
        dacc[p + a] = dacc[p + a] + (got[a * QPAD:(a + 1) * QPAD] + got[(2 + a) * QPAD:(3 + a) * QPAD])

    @pl.when(p == steps - 1)
    def _():
        for acc, table, out in ((gacc, down, grad_out), (dacc, down2, diag_out)):
            flat = acc[...].reshape(-1, comps * layers)
            head, tail = split(flat)
            out[...] = (jnp.dot(head, table[...], preferred_element_type=F32)
                        + jnp.dot(tail, table[...], preferred_element_type=F32))


def tile_terms(reference_tile, ext, nodal_field, offsets):
    rows, cols, layers = reference_tile.shape
    comps, ns, npx, nq = nodal_field.shape
    rim = rows // 4 + 1
    tabs = tables(rows, cols, layers, comps)
    nodes = jnp.pad(nodal_field.transpose(2, 3, 0, 1), ((0, 0), (0, QPAD - nq), (0, 0), (0, 0)))
    nodes = nodes.reshape(npx * QPAD, comps * ns)
    steps = rows // 8
    whole = lambda a: pl.BlockSpec(a.shape, lambda p, m: (0,) * a.ndim, pipeline_mode=pl.Buffered(1))
    slab = pl.BlockSpec((8, cols, layers), lambda p, m: (p, 0, 0))
    out_nodes = jax.ShapeDtypeStruct((npx * QPAD, 128), F32)
    grid_spec = pltpu.PrefetchScalarGridSpec(
        num_scalar_prefetch=1,
        grid=(steps,),
        in_specs=[slab, pl.BlockSpec(memory_space=pl.ANY), whole(nodes)] + [whole(t) for t in tabs],
        out_specs=[slab, whole(out_nodes), whole(out_nodes)],
        scratch_shapes=[
            pltpu.VMEM((rows + 2, cols + 2 * SIDE, layers), BF16),
            pltpu.VMEM((2 * cols, cols + 2 * SIDE), BF16),
            pltpu.VMEM((rows + 2, cols, layers), F32),
            pltpu.VMEM((npx, 2 * QPAD, comps * layers), BF16),
            pltpu.VMEM((8 * cols, comps * layers), F32),
            pltpu.VMEM((16, cols, layers), F32),
            pltpu.VMEM((8 * cols, layers), F32),
            pltpu.VMEM((2, 2 * cols, comps * layers), BF16),
            pltpu.VMEM((8 * cols, comps * layers), BF16),
            pltpu.VMEM((npx, QPAD, comps * layers), F32),
            pltpu.VMEM((npx, QPAD, comps * layers), F32),
            pltpu.SemaphoreType.DMA((steps + 1,)),
        ],
    )
    res, grad, diag = pl.pallas_call(
        functools.partial(tile_kernel, rim),
        grid_spec=grid_spec,
        out_shape=[jax.ShapeDtypeStruct(reference_tile.shape, BF16), out_nodes, out_nodes],
        compiler_params=pltpu.CompilerParams(
            dimension_semantics=("arbitrary",), vmem_limit_bytes=56 << 20),
        name="tile",
    )(offsets, reference_tile, ext, nodes, *tabs)
    back = lambda a: a.reshape(npx, QPAD, 128)[:, :nq, :comps * ns].reshape(npx, nq, comps, ns).transpose(2, 3, 0, 1)
    return res, back(grad), back(diag)


def element_energy(nodal_field):
    diff_x = nodal_field[:, :, 1:, :] - nodal_field[:, :, :-1, :]
    grad_x = 0.03125 * (
        diff_x[:, :-1, :, :-1]
        + diff_x[:, 1:, :, :-1]
        + diff_x[:, :-1, :, 1:]
        + diff_x[:, 1:, :, 1:]
    )
    diff_y = nodal_field[:, :, :, 1:] - nodal_field[:, :, :, :-1]
    grad_y = 0.03125 * (
        diff_y[:, :-1, :-1, :]
        + diff_y[:, 1:, :-1, :]
        + diff_y[:, :-1, 1:, :]
        + diff_y[:, 1:, 1:, :]
    )
    diff_z = nodal_field[:, 1:, :, :] - nodal_field[:, :-1, :, :]
    grad_z = 0.03125 * (
        diff_z[:, :, :-1, :-1]
        + diff_z[:, :, 1:, :-1]
        + diff_z[:, :, :-1, 1:]
        + diff_z[:, :, 1:, 1:]
    )
    columns = (grad_x, grad_y, grad_z)
    entries = [[columns[j][i] + (1.0 if i == j else 0.0) for j in range(3)] for i in range(3)]
    volume_ratio = (
        entries[0][0] * (entries[1][1] * entries[2][2] - entries[1][2] * entries[2][1])
        - entries[0][1] * (entries[1][0] * entries[2][2] - entries[1][2] * entries[2][0])
        + entries[0][2] * (entries[1][0] * entries[2][1] - entries[1][1] * entries[2][0])
    )
    squares = entries[0][0] * entries[0][0]
    for i in range(3):
        for j in range(3):
            if i + j > 0:
                squares = squares + entries[i][j] * entries[i][j]
    log_ratio = jnp.log(volume_ratio)
    energy = (
        0.5 * MU_SHEAR * (squares - 3.0 - 2.0 * log_ratio)
        + 0.5 * LAMBDA_BULK * log_ratio * log_ratio
    )
    return REG_WEIGHT * jnp.sum(energy)


def per_device(nw, nn, reference_image, deformed_image, displacement, tile_map):
    from_next = shifted(displacement[:, :, 0, :], "wide", -1)
    nodal_wide = jnp.concatenate([displacement, from_next[:, :, None, :]], axis=2)
    from_above = shifted(nodal_wide[:, :, :, 0], "narrow", -1)
    nodal_field = jnp.concatenate([nodal_wide, from_above[:, :, :, None]], axis=3)
    energy_value, energy_pull = jax.vjp(element_energy, nodal_field)
    reg_grad = energy_pull(jnp.ones_like(energy_value))[0]
    ext = exchange(deformed_image, nw, nn)
    residual, data_grad, data_diag = tile_terms(
        reference_image, ext, nodal_field, tile_map.reshape(2))
    both = jnp.stack([data_grad + reg_grad, data_diag])
    got_wide = shifted(both[:, :, :, -1, :], "wide", 1)
    both = both[:, :, :, :-1, :].at[:, :, :, 0, :].add(got_wide)
    got_narrow = shifted(both[:, :, :, :, -1], "narrow", 1)
    both = both[:, :, :, :, :-1].at[:, :, :, :, 0].add(got_narrow)
    updated = displacement - both[0] / (both[1] + STIFFNESS)
    return (updated, residual)


def solution(mesh):
    placed = (
        P("wide", "narrow", None),
        P("wide", "narrow", None),
        P(None, None, "wide", "narrow"),
        P("wide", "narrow", None),
    )
    return jax.shard_map(
        functools.partial(per_device, mesh.shape["wide"], mesh.shape["narrow"]),
        mesh=mesh,
        in_specs=placed,
        out_specs=(P(None, None, "wide", "narrow"), P("wide", "narrow", None)),
        check_vma=False,
    )
```

```python
import functools

import jax
import jax.numpy as jnp
import numpy as np
from jax import lax
from jax.experimental import pallas as pl
from jax.experimental.pallas import tpu as pltpu
from jax.sharding import PartitionSpec as P

MU_SHEAR = 1.0
LAMBDA_BULK = 2.0
REG_WEIGHT = 256.0
STIFFNESS = 16.0
MESH = pl.DeviceIdType.MESH
F32 = jnp.float32
BF16 = jnp.bfloat16
SIDE = 48
QPAD = 24


def as_int(flag):
    return flag.astype(jnp.int32)


def halo_kernel(nw, nn, rim, own, extra_in, edge_x, edge_y, ext, extra, edges,
                zeros, send, recv, zsem, lsem):
    rows, cols, _ = own.shape
    side = rim - 1
    w = lax.axis_index("wide")
    n = lax.axis_index("narrow")
    lo_w, hi_w, lo_n, hi_n = w > 0, w < nw - 1, n > 0, n < nn - 1
    up_w, dn_w = (w + 1, n), (w - 1, n)
    up_n, dn_n = (w, n + 1), (w, n - 1)
    mid = slice(side, side + cols)
    ylo = slice(0, side)
    yhi = slice(side + cols, 2 * side + cols)
    total = rows + 2 * rim
    emid = slice(SIDE, SIDE + rows)
    edges[...] = jnp.zeros_like(edges)
    extra[...] = jnp.zeros_like(extra)
    barrier = pltpu.get_barrier_semaphore()
    for there, device in ((lo_w, dn_w), (hi_w, up_w), (lo_n, dn_n), (hi_n, up_n)):
        @pl.when(there)
        def _(device=device):
            pl.semaphore_signal(barrier, inc=1, device_id=device, device_id_type=MESH)
    zeros[...] = jnp.zeros_like(zeros)
    jobs = []

    def fill(cond, dst):
        src = zeros.at[tuple(slice(0, d) for d in dst.shape)]
        jobs.append((cond, pltpu.make_async_copy(src, dst, zsem.at[len(jobs)])))

    for cond, span in ((jnp.logical_not(lo_n), ylo), (jnp.logical_not(hi_n), yhi)):
        fill(cond, ext.at[:, span])
    for cond, band in ((jnp.logical_not(lo_w), slice(0, rim)), (jnp.logical_not(hi_w), slice(rim + rows, total))):
        fill(cond, ext.at[band, mid])
        fill(cond & lo_n, ext.at[band, ylo])
        fill(cond & hi_n, ext.at[band, yhi])
    for cond, job in jobs:
        @pl.when(cond)
        def _(job=job):
            job.start()
    pl.semaphore_wait(barrier, as_int(lo_w) + as_int(hi_w) + as_int(lo_n) + as_int(hi_n))

    def remote(k, src, dst, device):
        return pltpu.make_async_remote_copy(
            src_ref=src, dst_ref=dst, send_sem=send.at[k], recv_sem=recv.at[k],
            device_id=device, device_id_type=MESH)

    first = [
        (lo_w, hi_w, remote(0, edge_x, edges.at[0], dn_w)),
        (lo_n, hi_n, remote(1, edge_y, edges.at[1], dn_n)),
        (hi_n, lo_n, remote(2, extra_in.at[0], extra.at[0, emid], up_n)),
        (lo_n, hi_n, remote(3, extra_in.at[1], extra.at[1, emid], dn_n)),
    ]
    full = (slice(0, rim), slice(rows - rim, rows), slice(rim, rows - rim))
    for j, part in enumerate(full):
        there = slice(part.start + rim, part.stop + rim)
        first.append((hi_n, lo_n, remote(4 + 2 * j, own.at[part, cols - side:cols], ext.at[there, ylo], up_n)))
        first.append((lo_n, hi_n, remote(5 + 2 * j, own.at[part, 0:side], ext.at[there, yhi], dn_n)))
    first.append((hi_w, lo_w, remote(10, own.at[rows - rim:rows], ext.at[0:rim, mid], up_w)))
    first.append((lo_w, hi_w, remote(11, own.at[0:rim], ext.at[rows + rim:total, mid], dn_w)))
    for goes, _c, copy in first:
        @pl.when(goes)
        def _(copy=copy):
            copy.start()
    local = pltpu.make_async_copy(own, ext.at[rim:rim + rows, mid], lsem)
    local.start()
    low_rows, high_rows = slice(rim, 2 * rim), slice(rows, rows + rim)
    below, above = slice(0, rim), slice(rim + rows, total)
    elow, ehigh = slice(SIDE, 2 * SIDE), slice(rows, SIDE + rows)
    ebelow, eabove = slice(0, SIDE), slice(SIDE + rows, 2 * SIDE + rows)
    second = {
        0: [(hi_w & lo_n, hi_w & hi_n, remote(12, edges.at[0], edges.at[2], dn_n))],
        2: [(lo_n & lo_w, lo_n & hi_w, remote(13, extra.at[0, elow], extra.at[0, eabove], dn_w)),
            (lo_n & hi_w, lo_n & lo_w, remote(14, extra.at[0, ehigh], extra.at[0, ebelow], up_w))],
        3: [(hi_n & lo_w, hi_n & hi_w, remote(15, extra.at[1, elow], extra.at[1, eabove], dn_w)),
            (hi_n & hi_w, hi_n & lo_w, remote(16, extra.at[1, ehigh], extra.at[1, ebelow], up_w))],
        4: [(lo_n & lo_w, lo_n & hi_w, remote(17, ext.at[low_rows, ylo], ext.at[above, ylo], dn_w))],
        5: [(hi_n & lo_w, hi_n & hi_w, remote(18, ext.at[low_rows, yhi], ext.at[above, yhi], dn_w))],
        6: [(lo_n & hi_w, lo_n & lo_w, remote(19, ext.at[high_rows, ylo], ext.at[below, ylo], up_w))],
        7: [(hi_n & hi_w, hi_n & lo_w, remote(20, ext.at[high_rows, yhi], ext.at[below, yhi], up_w))],
    }
    later = []
    for k, (_g, comes, copy) in enumerate(first):
        @pl.when(comes)
        def _(copy=copy):
            copy.wait_recv()
        for entry in second.get(k, ()):
            later.append(entry)
            @pl.when(entry[0])
            def _(entry=entry):
                entry[2].start()
    for _g, comes, copy in later:
        @pl.when(comes)
        def _(copy=copy):
            copy.wait_recv()
    for goes, _c, copy in first + later:
        @pl.when(goes)
        def _(copy=copy):
            copy.wait_send()
    for cond, job in jobs:
        @pl.when(cond)
        def _(job=job):
            job.wait()
    local.wait()


def exchange(deformed, by_node, nw, nn):
    rows, cols, layers = deformed.shape
    rim = rows // 4 + 1
    shape = (rows + 2 * rim, cols + 2 * (rim - 1), layers)
    extra_in = jnp.stack([deformed[:, cols - rim], deformed[:, rim - 1]])
    anywhere = pl.BlockSpec(memory_space=pl.ANY)
    near = pl.BlockSpec(memory_space=pltpu.VMEM)
    lanes = by_node.shape[-1]
    return pl.pallas_call(
        functools.partial(halo_kernel, nw, nn, rim),
        out_shape=[jax.ShapeDtypeStruct(shape, BF16),
                   jax.ShapeDtypeStruct((2, rows + 2 * SIDE, layers), BF16),
                   jax.ShapeDtypeStruct((3,) + by_node.shape[1:], F32)],
        in_specs=[anywhere, near, near, near],
        out_specs=[anywhere, near, near],
        scratch_shapes=[
            pltpu.VMEM((shape[0], cols, layers), BF16),
            pltpu.SemaphoreType.DMA((21,)),
            pltpu.SemaphoreType.DMA((21,)),
            pltpu.SemaphoreType.DMA((8,)),
            pltpu.SemaphoreType.DMA,
        ],
        compiler_params=pltpu.CompilerParams(
            collective_id=0, has_side_effects=True, vmem_limit_bytes=62 << 20),
        name="halo",
    )(deformed, extra_in, by_node[0], by_node[:, 0])


def tables(rows, cols, layers, comps):
    def one(voxels):
        t = np.zeros((voxels, voxels // 8 + 1))
        for i in range(voxels):
            f = (i % 8 + 0.5) / 8.0
            t[i, i // 8] += 1.0 - f
            t[i, i // 8 + 1] += f
        return t
    ty, tz = one(cols), one(layers)
    nq, ns = ty.shape[1], tz.shape[1]
    typ = np.zeros((cols, QPAD))
    typ[:, :nq] = ty
    frac = (np.arange(8) + 0.5) / 8.0
    wx = np.stack([1.0 - frac, frac], 1)
    inter = 0.5 * np.einsum("ka,yq->kyaq", wx, typ)
    inter = np.concatenate([inter[:, :, 0], inter[:, :, 0], inter[:, :, 1], inter[:, :, 1]], -1)
    inter = inter.reshape(8 * cols, 4 * QPAD)
    proj = np.concatenate([typ.T, typ.T], 1)
    diag = np.einsum("ka,yq->aqky", wx * wx, typ * typ).reshape(2 * QPAD, 8 * cols)
    dhi = diag.astype(BF16).astype(np.float64)
    diag = np.concatenate([dhi, diag - dhi], 0)
    lanes = comps * layers
    up = np.zeros((2 * 128, lanes))
    down = np.zeros((lanes, 128))
    down2 = np.zeros((lanes, 128))
    for c in range(comps):
        for h in range(2):
            up[h * 128 + c * ns:h * 128 + (c + 1) * ns, c * layers:(c + 1) * layers] = tz.T
        down[c * layers:(c + 1) * layers, c * ns:(c + 1) * ns] = -0.5 * tz
        down2[c * layers:(c + 1) * layers, c * ns:(c + 1) * ns] = 0.25 * tz * tz
    dz = np.zeros((layers, layers))
    for z in range(layers):
        if z + 1 < layers:
            dz[z + 1, z] = 1.0
        if z > 0:
            dz[z - 1, z] = -1.0
    as_bf16 = lambda a: jnp.asarray(a.astype(BF16))
    return [as_bf16(a) for a in (inter, proj, diag, up, down, down2, dz)]


def split(value):
    high = value.astype(BF16)
    return high, (value - high.astype(F32)).astype(BF16)


def strain_pull(ns, nodes, pull):
    npx = nodes.shape[0]
    nel = npx - 1
    lane = lax.broadcasted_iota(jnp.int32, (nel, 128), 1)
    move = lambda a, by: pltpu.roll(a, by % 128, 1)
    pull[...] = jnp.zeros_like(pull)

    @pl.loop(0, nel)
    def _(p):
        a00, a01 = nodes[p, 0:nel], nodes[p, 1:nel + 1]
        a10, a11 = nodes[p + 1, 0:nel], nodes[p + 1, 1:nel + 1]
        dx = (a10 - a00) + (a11 - a01)
        dy = (a01 - a00) + (a11 - a10)
        every = (a00 + a01) + (a10 + a11)
        slopes = (dx + move(dx, -1), dy + move(dy, -1), move(every, -1) - every)
        f = [[0.03125 * (move(h, -ns * i) if i else h) + (1.0 if i == j else 0.0)
              for j, h in enumerate(slopes)] for i in range(3)]
        cof = [[f[(i + 1) % 3][(j + 1) % 3] * f[(i + 2) % 3][(j + 2) % 3]
                - f[(i + 1) % 3][(j + 2) % 3] * f[(i + 2) % 3][(j + 1) % 3]
                for j in range(3)] for i in range(3)]
        ratio = f[0][0] * cof[0][0] + f[0][1] * cof[0][1] + f[0][2] * cof[0][2]
        factor = (LAMBDA_BULK * jnp.log(ratio) - MU_SHEAR) / ratio
        back = []
        for j in range(3):
            parts = [jnp.where(lane < ns - 1, MU_SHEAR * f[i][j] + factor * cof[i][j], 0.0) for i in range(3)]
            back.append((parts[0] + move(parts[1], ns) + move(parts[2], 2 * ns)) * (0.03125 * REG_WEIGHT))
        gx = back[0] + move(back[0], 1)
        gy = back[1] + move(back[1], 1)
        gz = move(back[2], 1) - back[2]
        for dp, dq in ((0, 0), (0, 1), (1, 0), (1, 1)):
            add = (gx if dp else -gx) + (gy if dq else -gy) + gz
            pull[p + dp, dq:dq + nel] = pull[p + dp, dq:dq + nel] + add


def tile_kernel(rim, ns, map_ref, ref_tile, ext, extra, by_node, edges,
                inter, proj, diag, up, down, down2, dz,
                res, out,
                rows_in, shift, samp, ndz, moved, gy, gz, sums, sq, gacc, dacc, nodes, pull, rimcol, sem):
    p = pl.program_id(0)
    steps = pl.num_programs(0)
    cols, layers = samp.shape[1], samp.shape[2]
    comps = ndz.shape[2] // layers
    side = rim - 1
    wide_cols = cols + 2 * side
    start = map_ref[0] + side

    def fetch(first, count, k):
        return pltpu.make_async_copy(
            ext.at[pl.ds(start + first, count)],
            rows_in.at[pl.ds(first, count), 0:wide_cols], sem.at[k])

    def sample(first, count):
        for a in range(count):
            at = map_ref[0] + (SIDE - 1) + first + a
            which = lax.broadcasted_iota(jnp.int32, (16, layers), 0)
            low = jnp.broadcast_to(rimcol[0, pl.ds(at, 1), :], (16, layers))
            high = jnp.broadcast_to(rimcol[1, pl.ds(at, 1), :], (16, layers))
            rows_in[first + a, wide_cols:wide_cols + 16] = jnp.where(
                which == 0, low, jnp.where(which == 1, high, 0.0)).astype(BF16)
        for a in range(0, count, 2):
            pair = jnp.concatenate([rows_in[first + a], rows_in[first + a + 1]], axis=1)
            got = jnp.dot(shift[...], pair, preferred_element_type=F32)
            for b in range(2):
                samp[first + a + b] = got[:cols, b * layers:(b + 1) * layers]
                gy[(first + a + b) % 16] = got[cols:, b * layers:(b + 1) * layers]

    @pl.when(p == 0)
    def _():
        fetch(0, 2, steps).start()

        @pl.loop(0, steps)
        def _(k):
            fetch(8 * k + 2, 8, k).start()
        rimcol[...] = extra[...].astype(F32)
        y = lax.broadcasted_iota(jnp.int32, (cols, shift.shape[1]), 0)
        k = lax.broadcasted_iota(jnp.int32, (cols, shift.shape[1]), 1)
        place = jnp.where(k < wide_cols, k - side,
                          jnp.where(k == wide_cols, -side - 1,
                                    jnp.where(k == wide_cols + 1, cols + side, 1 << 20)))
        gap = place - y - map_ref[1]
        shift[:cols] = jnp.where(gap == 0, 1.0, 0.0).astype(BF16)
        shift[cols:] = (jnp.where(gap == 1, 1.0, 0.0) - jnp.where(gap == -1, 1.0, 0.0)).astype(BF16)
        nel = by_node.shape[0]
        nodes[0:nel, 0:nel] = by_node[...]
        nodes[nel, 0:nel] = edges[0]
        top = lax.broadcasted_iota(jnp.int32, (QPAD - nel, 128), 0) == 0
        for i in range(nel + 1):
            row = edges[1, i:i + 1] if i < nel else edges[2, 0:1]
            nodes[i, nel:QPAD] = jnp.where(top, jnp.broadcast_to(row, (QPAD - nel, 128)), 0.0)
        flat = nodes[...].reshape(-1, 128)
        high = flat.astype(BF16).astype(F32)
        both = jnp.concatenate([high, flat - high], axis=1).astype(BF16)
        level = jnp.dot(both, up[...], preferred_element_type=F32)
        for i in range(ndz.shape[0]):
            part = level[i * QPAD:(i + 1) * QPAD]
            head = part.astype(BF16).astype(F32)
            ndz[i] = jnp.concatenate([head, part - head], axis=0).astype(BF16)
        strain_pull(ns, nodes, pull)
        gacc[...] = jnp.zeros_like(gacc)
        dacc[...] = jnp.zeros_like(dacc)
        fetch(0, 2, steps).wait()
        sample(0, 2)

    base = pl.multiple_of(8 * p, 8)
    fetch(base + 2, 8, p).wait()
    sample(base + 2, 8)
    gz[...] = jnp.dot(samp[pl.ds(base + 1, 8)].reshape(8 * cols, layers).astype(BF16), dz[...],
                      preferred_element_type=F32)
    level = ndz[pl.ds(p, 2)].reshape(4 * QPAD, comps * layers)
    moved[...] = jnp.dot(inter[...], level, preferred_element_type=F32)

    chunk = 32

    @pl.loop(0, cols // chunk)
    def _(j):
        at = pl.multiple_of(j * chunk, chunk)
        span = pl.ds(at, chunk)
        run = [None] * comps
        tot = [None] * comps
        for k in range(8):
            line = pl.ds(k * cols + at, chunk)
            here = samp[base + 1 + k, span, :]
            g = [samp[base + 2 + k, span, :] - samp[base + k, span, :],
                 gy[(base + 1 + k) % 16, span, :],
                 gz[line, :]]
            r = ref_tile[k, span, :].astype(F32) - here
            for c in range(3):
                r = r - g[c] * moved[line, c * layers:(c + 1) * layers]
            res[k, span, :] = r.astype(BF16)
            for c in range(3):
                f = g[c] * r
                run[c] = f if k == 0 else run[c] + f
                tot[c] = run[c] if k == 0 else tot[c] + run[c]
                sq[line, c * layers:(c + 1) * layers] = (g[c] * g[c]).astype(BF16)
        for c in range(3):
            low = (tot[c] - 0.5 * run[c]) * 0.125
            for a, value in enumerate((low, run[c] - low)):
                head, tail = split(value)
                sums[a, span, c * layers:(c + 1) * layers] = head
                sums[a, pl.ds(cols + at, chunk), c * layers:(c + 1) * layers] = tail

    for a in range(2):
        gacc[p + a] = gacc[p + a] + jnp.dot(proj[...], sums[a], preferred_element_type=F32)
    got = jnp.dot(diag[...], sq[...], preferred_element_type=F32)
    for a in range(2):
        dacc[p + a] = dacc[p + a] + (got[a * QPAD:(a + 1) * QPAD] + got[(2 + a) * QPAD:(3 + a) * QPAD])

    @pl.when(p == steps - 1)
    def _():
        for k, (acc, table) in enumerate(((gacc, down), (dacc, down2))):
            head, tail = split(acc[...].reshape(-1, comps * layers))
            got = (jnp.dot(head, table[...], preferred_element_type=F32)
                   + jnp.dot(tail, table[...], preferred_element_type=F32)).reshape(pull.shape)
            out[k] = got + pull[...] if k == 0 else got


def tile_terms(reference_tile, ext, extra, by_node, edges, offsets, ns):
    rows, cols, layers = reference_tile.shape
    comps = 3
    npx = by_node.shape[0] + 1
    rim = rows // 4 + 1
    tabs = tables(rows, cols, layers, comps)
    steps = rows // 8
    whole = lambda a: pl.BlockSpec(a.shape, lambda p, m: (0,) * a.ndim, pipeline_mode=pl.Buffered(1))
    slab = pl.BlockSpec((8, cols, layers), lambda p, m: (p, 0, 0))
    out_nodes = jax.ShapeDtypeStruct((2, npx, QPAD, 128), F32)
    depth = cols + 2 * (rim - 1) + 16
    grid_spec = pltpu.PrefetchScalarGridSpec(
        num_scalar_prefetch=1,
        grid=(steps,),
        in_specs=[slab, pl.BlockSpec(memory_space=pl.ANY), whole(extra), whole(by_node), whole(edges)]
        + [whole(t) for t in tabs],
        out_specs=[slab, whole(out_nodes)],
        scratch_shapes=[
            pltpu.VMEM((rows + 2, depth, layers), BF16),
            pltpu.VMEM((2 * cols, depth), BF16),
            pltpu.VMEM((rows + 2, cols, layers), F32),
            pltpu.VMEM((npx, 2 * QPAD, comps * layers), BF16),
            pltpu.VMEM((8 * cols, comps * layers), F32),
            pltpu.VMEM((16, cols, layers), F32),
            pltpu.VMEM((8 * cols, layers), F32),
            pltpu.VMEM((2, 2 * cols, comps * layers), BF16),
            pltpu.VMEM((8 * cols, comps * layers), BF16),
            pltpu.VMEM((npx, QPAD, comps * layers), F32),
            pltpu.VMEM((npx, QPAD, comps * layers), F32),
            pltpu.VMEM((npx, QPAD, 128), F32),
            pltpu.VMEM((npx, QPAD, 128), F32),
            pltpu.VMEM(extra.shape, F32),
            pltpu.SemaphoreType.DMA((steps + 1,)),
        ],
    )
    return pl.pallas_call(
        functools.partial(tile_kernel, rim, ns),
        grid_spec=grid_spec,
        out_shape=[jax.ShapeDtypeStruct(reference_tile.shape, BF16), out_nodes],
        compiler_params=pltpu.CompilerParams(
            dimension_semantics=("arbitrary",), vmem_limit_bytes=62 << 20),
        name="tile",
    )(offsets, reference_tile, ext, extra, by_node, edges, *tabs)


def node_kernel(nw, nn, terms, by_node, out, column, from_w, from_n, from_c, send, recv):
    nel = by_node.shape[0]
    w = lax.axis_index("wide")
    n = lax.axis_index("narrow")
    lo_w, hi_w, lo_n, hi_n = w > 0, w < nw - 1, n > 0, n < nn - 1
    up_w, dn_w = (w + 1, n), (w - 1, n)
    up_n, dn_n = (w, n + 1), (w, n - 1)
    for ref in (from_w, from_n, from_c):
        ref[...] = jnp.zeros_like(ref)
    barrier = pltpu.get_barrier_semaphore()
    for there, device in ((lo_w, dn_w), (hi_w, up_w), (lo_n, dn_n), (hi_n, up_n)):
        @pl.when(there)
        def _(device=device):
            pl.semaphore_signal(barrier, inc=1, device_id=device, device_id_type=MESH)
    for k in range(2):
        for p in range(nel):
            column[k, p:p + 1] = terms[k, p, nel:nel + 1]
    pl.semaphore_wait(barrier, as_int(lo_w) + as_int(hi_w) + as_int(lo_n) + as_int(hi_n))

    def remote(k, src, dst, device):
        return pltpu.make_async_remote_copy(
            src_ref=src, dst_ref=dst, send_sem=send.at[k], recv_sem=recv.at[k],
            device_id=device, device_id_type=MESH)

    wide_copy = remote(0, terms.at[:, nel], from_w, up_w)
    narrow_copy = remote(1, column, from_n, up_n)
    corner_copy = remote(2, from_w.at[:, nel:QPAD], from_c, up_n)

    @pl.when(hi_w)
    def _():
        wide_copy.start()

    @pl.when(hi_n)
    def _():
        narrow_copy.start()

    @pl.when(lo_w)
    def _():
        wide_copy.wait_recv()

    @pl.when(lo_w & hi_n)
    def _():
        corner_copy.start()

    @pl.when(lo_n)
    def _():
        narrow_copy.wait_recv()

    @pl.when(lo_w & lo_n)
    def _():
        corner_copy.wait_recv()

    top = lax.broadcasted_iota(jnp.int32, (nel, 128), 0) == 0
    for p in range(nel):
        sums = []
        for k in range(2):
            value = terms[k, p, 0:nel]
            side = from_n[k, p:p + 1]
            if p == 0:
                value = value + from_w[k, 0:nel]
                side = side + from_c[k, 0:1]
            sums.append(value + jnp.where(top, jnp.broadcast_to(side, (nel, 128)), 0.0))
        out[p] = by_node[p] - sums[0] / (sums[1] + STIFFNESS)

    @pl.when(hi_w)
    def _():
        wide_copy.wait_send()

    @pl.when(hi_n)
    def _():
        narrow_copy.wait_send()

    @pl.when(lo_w & hi_n)
    def _():
        corner_copy.wait_send()


def node_update(terms, by_node, nw, nn):
    nel = by_node.shape[0]
    near = pl.BlockSpec(memory_space=pltpu.VMEM)
    return pl.pallas_call(
        functools.partial(node_kernel, nw, nn),
        out_shape=jax.ShapeDtypeStruct(by_node.shape, F32),
        in_specs=[near, near],
        out_specs=near,
        scratch_shapes=[
            pltpu.VMEM((2, nel, 128), F32),
            pltpu.VMEM((2, QPAD, 128), F32),
            pltpu.VMEM((2, nel, 128), F32),
            pltpu.VMEM((2, QPAD - nel, 128), F32),
            pltpu.SemaphoreType.DMA((3,)),
            pltpu.SemaphoreType.DMA((3,)),
        ],
        compiler_params=pltpu.CompilerParams(collective_id=1, has_side_effects=True),
        name="nodes",
    )(terms, by_node)


def per_device(nw, nn, reference_image, deformed_image, displacement, tile_map):
    comps, ns, nex, ney = displacement.shape
    by_node = displacement.transpose(2, 3, 0, 1).reshape(nex, ney, comps * ns)
    by_node = jnp.pad(by_node, ((0, 0), (0, 0), (0, 128 - comps * ns)))
    ext, extra, edges = exchange(deformed_image, by_node, nw, nn)
    residual, terms = tile_terms(
        reference_image, ext, extra, by_node, edges, tile_map.reshape(2), ns)
    moved = node_update(terms, by_node, nw, nn)
    updated = moved[:, :, :comps * ns].reshape(nex, ney, comps, ns).transpose(2, 3, 0, 1)
    return (updated, residual)


def solution(mesh):
    placed = (
        P("wide", "narrow", None),
        P("wide", "narrow", None),
        P(None, None, "wide", "narrow"),
        P("wide", "narrow", None),
    )
    return jax.shard_map(
        functools.partial(per_device, mesh.shape["wide"], mesh.shape["narrow"]),
        mesh=mesh,
        in_specs=placed,
        out_specs=(P(None, None, "wide", "narrow"), P("wide", "narrow", None)),
        check_vma=False,
    )
```

```python
import functools

import jax
import jax.numpy as jnp
import numpy as np
from jax import lax
from jax.experimental import pallas as pl
from jax.experimental.pallas import tpu as pltpu
from jax.sharding import PartitionSpec as P

MU_SHEAR = 1.0
LAMBDA_BULK = 2.0
REG_WEIGHT = 256.0
STIFFNESS = 16.0
MESH = pl.DeviceIdType.MESH
F32 = jnp.float32
BF16 = jnp.bfloat16
SIDE = 48
QPAD = 24


def as_int(flag):
    return flag.astype(jnp.int32)


def halo_kernel(nw, nn, rim, own, extra_in, edge_x, edge_y, out, extra, edges,
                ext, zeros, send, recv, zsem, lsem):
    rows, cols, _ = own.shape
    side = rim - 1
    w = lax.axis_index("wide")
    n = lax.axis_index("narrow")
    lo_w, hi_w, lo_n, hi_n = w > 0, w < nw - 1, n > 0, n < nn - 1
    up_w, dn_w = (w + 1, n), (w - 1, n)
    up_n, dn_n = (w, n + 1), (w, n - 1)
    mid = slice(side, side + cols)
    ylo = slice(0, side)
    yhi = slice(side + cols, 2 * side + cols)
    total = rows + 2 * rim
    emid = slice(SIDE, SIDE + rows)
    local = pltpu.make_async_copy(own, ext.at[rim:rim + rows, mid], lsem.at[0])
    local.start()
    edges[...] = jnp.zeros_like(edges)
    extra[...] = jnp.zeros_like(extra)
    barrier = pltpu.get_barrier_semaphore()
    for there, device in ((lo_w, dn_w), (hi_w, up_w), (lo_n, dn_n), (hi_n, up_n)):
        @pl.when(there)
        def _(device=device):
            pl.semaphore_signal(barrier, inc=1, device_id=device, device_id_type=MESH)
    zeros[...] = jnp.zeros_like(zeros)
    jobs = []

    def fill(cond, dst):
        src = zeros.at[tuple(slice(0, d) for d in dst.shape)]
        jobs.append((cond, pltpu.make_async_copy(src, dst, zsem.at[len(jobs)])))

    for cond, span in ((jnp.logical_not(lo_n), ylo), (jnp.logical_not(hi_n), yhi)):
        fill(cond, ext.at[:, span])
    for cond, band in ((jnp.logical_not(lo_w), slice(0, rim)), (jnp.logical_not(hi_w), slice(rim + rows, total))):
        fill(cond, ext.at[band, mid])
        fill(cond & lo_n, ext.at[band, ylo])
        fill(cond & hi_n, ext.at[band, yhi])
    for cond, job in jobs:
        @pl.when(cond)
        def _(job=job):
            job.start()
    pl.semaphore_wait(barrier, as_int(lo_w) + as_int(hi_w) + as_int(lo_n) + as_int(hi_n))

    def remote(k, src, dst, device):
        return pltpu.make_async_remote_copy(
            src_ref=src, dst_ref=dst, send_sem=send.at[k], recv_sem=recv.at[k],
            device_id=device, device_id_type=MESH)

    first = [
        (lo_w, hi_w, remote(0, edge_x, edges.at[0], dn_w)),
        (lo_n, hi_n, remote(1, edge_y, edges.at[1], dn_n)),
        (hi_n, lo_n, remote(2, extra_in.at[0], extra.at[0, emid], up_n)),
        (lo_n, hi_n, remote(3, extra_in.at[1], extra.at[1, emid], dn_n)),
    ]
    full = (slice(0, rim), slice(rows - rim, rows), slice(rim, rows - rim))
    for j, part in enumerate(full):
        there = slice(part.start + rim, part.stop + rim)
        first.append((hi_n, lo_n, remote(4 + 2 * j, ext.at[there, cols:cols + side], ext.at[there, ylo], up_n)))
        first.append((lo_n, hi_n, remote(5 + 2 * j, ext.at[there, side:2 * side], ext.at[there, yhi], dn_n)))
    first.append((hi_w, lo_w, remote(10, ext.at[rows:rows + rim, mid], ext.at[0:rim, mid], up_w)))
    first.append((lo_w, hi_w, remote(11, ext.at[rim:2 * rim, mid], ext.at[rows + rim:total, mid], dn_w)))
    local.wait()
    saves = []

    def settle(k, span, columns):
        save = pltpu.make_async_copy(ext.at[span, columns], out.at[span, columns], lsem.at[1 + k])
        save.start()
        saves.append(save)

    for goes, _c, copy in first:
        @pl.when(goes)
        def _(copy=copy):
            copy.start()
    settle(0, slice(rim, rim + rows), mid)
    low_rows, high_rows = slice(rim, 2 * rim), slice(rows, rows + rim)
    below, above = slice(0, rim), slice(rim + rows, total)
    elow, ehigh = slice(SIDE, 2 * SIDE), slice(rows, SIDE + rows)
    ebelow, eabove = slice(0, SIDE), slice(SIDE + rows, 2 * SIDE + rows)
    second = {
        0: [(hi_w & lo_n, hi_w & hi_n, remote(12, edges.at[0], edges.at[2], dn_n))],
        2: [(lo_n & lo_w, lo_n & hi_w, remote(13, extra.at[0, elow], extra.at[0, eabove], dn_w)),
            (lo_n & hi_w, lo_n & lo_w, remote(14, extra.at[0, ehigh], extra.at[0, ebelow], up_w))],
        3: [(hi_n & lo_w, hi_n & hi_w, remote(15, extra.at[1, elow], extra.at[1, eabove], dn_w)),
            (hi_n & hi_w, hi_n & lo_w, remote(16, extra.at[1, ehigh], extra.at[1, ebelow], up_w))],
        4: [(lo_n & lo_w, lo_n & hi_w, remote(17, ext.at[low_rows, ylo], ext.at[above, ylo], dn_w))],
        5: [(hi_n & lo_w, hi_n & hi_w, remote(18, ext.at[low_rows, yhi], ext.at[above, yhi], dn_w))],
        6: [(lo_n & hi_w, lo_n & lo_w, remote(19, ext.at[high_rows, ylo], ext.at[below, ylo], up_w))],
        7: [(hi_n & hi_w, hi_n & lo_w, remote(20, ext.at[high_rows, yhi], ext.at[below, yhi], up_w))],
    }
    later = []
    for k, (_g, comes, copy) in enumerate(first):
        @pl.when(comes)
        def _(copy=copy):
            copy.wait_recv()
        for entry in second.get(k, ()):
            later.append(entry)
            @pl.when(entry[0])
            def _(entry=entry):
                entry[2].start()
    for _g, comes, copy in later:
        @pl.when(comes)
        def _(copy=copy):
            copy.wait_recv()
    for cond, job in jobs:
        @pl.when(cond)
        def _(job=job):
            job.wait()
    settle(1, below, mid)
    settle(2, above, mid)
    settle(3, slice(0, total), ylo)
    settle(4, slice(0, total), yhi)
    for goes, _c, copy in first + later:
        @pl.when(goes)
        def _(copy=copy):
            copy.wait_send()
    for save in saves:
        save.wait()


def exchange(deformed, by_node, nw, nn):
    rows, cols, layers = deformed.shape
    rim = rows // 4 + 1
    shape = (rows + 2 * rim, cols + 2 * (rim - 1), layers)
    extra_in = jnp.stack([deformed[:, cols - rim], deformed[:, rim - 1]])
    anywhere = pl.BlockSpec(memory_space=pl.ANY)
    near = pl.BlockSpec(memory_space=pltpu.VMEM)
    lanes = by_node.shape[-1]
    return pl.pallas_call(
        functools.partial(halo_kernel, nw, nn, rim),
        out_shape=[jax.ShapeDtypeStruct(shape, BF16),
                   jax.ShapeDtypeStruct((2, rows + 2 * SIDE, layers), BF16),
                   jax.ShapeDtypeStruct((3,) + by_node.shape[1:], F32)],
        in_specs=[anywhere, near, near, near],
        out_specs=[anywhere, near, near],
        scratch_shapes=[
            pltpu.VMEM(shape, BF16),
            pltpu.VMEM((shape[0], cols, layers), BF16),
            pltpu.SemaphoreType.DMA((21,)),
            pltpu.SemaphoreType.DMA((21,)),
            pltpu.SemaphoreType.DMA((8,)),
            pltpu.SemaphoreType.DMA((6,)),
        ],
        compiler_params=pltpu.CompilerParams(
            collective_id=0, has_side_effects=True, vmem_limit_bytes=62 << 20),
        name="halo",
    )(deformed, extra_in, by_node[0], by_node[:, 0])


def tables(rows, cols, layers, comps):
    def one(voxels):
        t = np.zeros((voxels, voxels // 8 + 1))
        for i in range(voxels):
            f = (i % 8 + 0.5) / 8.0
            t[i, i // 8] += 1.0 - f
            t[i, i // 8 + 1] += f
        return t
    ty, tz = one(cols), one(layers)
    nq, ns = ty.shape[1], tz.shape[1]
    typ = np.zeros((cols, QPAD))
    typ[:, :nq] = ty
    frac = (np.arange(8) + 0.5) / 8.0
    wx = np.stack([1.0 - frac, frac], 1)
    inter = 0.5 * np.einsum("ka,yq->kyaq", wx, typ)
    inter = np.concatenate([inter[:, :, 0], inter[:, :, 0], inter[:, :, 1], inter[:, :, 1]], -1)
    inter = inter.reshape(8 * cols, 4 * QPAD)
    proj = np.concatenate([typ.T, typ.T], 1)
    diag = np.einsum("ka,yq->aqky", wx * wx, typ * typ).reshape(2 * QPAD, 8 * cols)
    dhi = diag.astype(BF16).astype(np.float64)
    diag = np.concatenate([dhi, diag - dhi], 0)
    lanes = comps * layers
    up = np.zeros((2 * 128, lanes))
    down = np.zeros((lanes, 128))
    down2 = np.zeros((lanes, 128))
    for c in range(comps):
        for h in range(2):
            up[h * 128 + c * ns:h * 128 + (c + 1) * ns, c * layers:(c + 1) * layers] = tz.T
        down[c * layers:(c + 1) * layers, c * ns:(c + 1) * ns] = -0.5 * tz
        down2[c * layers:(c + 1) * layers, c * ns:(c + 1) * ns] = 0.25 * tz * tz
    dz = np.zeros((layers, layers))
    for z in range(layers):
        if z + 1 < layers:
            dz[z + 1, z] = 1.0
        if z > 0:
            dz[z - 1, z] = -1.0
    as_bf16 = lambda a: jnp.asarray(a.astype(BF16))
    return [as_bf16(a) for a in (inter, proj, diag, up, down, down2, dz)]


def split(value):
    high = value.astype(BF16)
    return high, (value - high.astype(F32)).astype(BF16)


def strain_pull(ns, nodes, pull):
    npx = nodes.shape[0]
    nel = npx - 1
    lane = lax.broadcasted_iota(jnp.int32, (nel, 128), 1)
    move = lambda a, by: pltpu.roll(a, by % 128, 1)
    pull[...] = jnp.zeros_like(pull)

    @pl.loop(0, nel)
    def _(p):
        a00, a01 = nodes[p, 0:nel], nodes[p, 1:nel + 1]
        a10, a11 = nodes[p + 1, 0:nel], nodes[p + 1, 1:nel + 1]
        dx = (a10 - a00) + (a11 - a01)
        dy = (a01 - a00) + (a11 - a10)
        every = (a00 + a01) + (a10 + a11)
        slopes = (dx + move(dx, -1), dy + move(dy, -1), move(every, -1) - every)
        f = [[0.03125 * (move(h, -ns * i) if i else h) + (1.0 if i == j else 0.0)
              for j, h in enumerate(slopes)] for i in range(3)]
        cof = [[f[(i + 1) % 3][(j + 1) % 3] * f[(i + 2) % 3][(j + 2) % 3]
                - f[(i + 1) % 3][(j + 2) % 3] * f[(i + 2) % 3][(j + 1) % 3]
                for j in range(3)] for i in range(3)]
        ratio = f[0][0] * cof[0][0] + f[0][1] * cof[0][1] + f[0][2] * cof[0][2]
        factor = (LAMBDA_BULK * jnp.log(ratio) - MU_SHEAR) / ratio
        back = []
        for j in range(3):
            parts = [jnp.where(lane < ns - 1, MU_SHEAR * f[i][j] + factor * cof[i][j], 0.0) for i in range(3)]
            back.append((parts[0] + move(parts[1], ns) + move(parts[2], 2 * ns)) * (0.03125 * REG_WEIGHT))
        gx = back[0] + move(back[0], 1)
        gy = back[1] + move(back[1], 1)
        gz = move(back[2], 1) - back[2]
        for dp, dq in ((0, 0), (0, 1), (1, 0), (1, 1)):
            add = (gx if dp else -gx) + (gy if dq else -gy) + gz
            pull[p + dp, dq:dq + nel] = pull[p + dp, dq:dq + nel] + add


def tile_kernel(rim, ns, map_ref, ref_tile, ext, extra, by_node, edges,
                inter, proj, diag, up, down, down2, dz,
                res, out,
                rows_in, shift, samp, ndz, moved, gy, gz, sums, sq, gacc, dacc, nodes, pull, rimcol, sem):
    p = pl.program_id(0)
    steps = pl.num_programs(0)
    cols, layers = samp.shape[1], samp.shape[2]
    comps = ndz.shape[2] // layers
    side = rim - 1
    wide_cols = cols + 2 * side
    start = map_ref[0] + side

    def fetch(first, count, k):
        return pltpu.make_async_copy(
            ext.at[pl.ds(start + first, count)],
            rows_in.at[pl.ds(first, count), 0:wide_cols], sem.at[k])

    def sample(first, count):
        for a in range(count):
            at = map_ref[0] + (SIDE - 1) + first + a
            which = lax.broadcasted_iota(jnp.int32, (16, layers), 0)
            low = jnp.broadcast_to(rimcol[0, pl.ds(at, 1), :], (16, layers))
            high = jnp.broadcast_to(rimcol[1, pl.ds(at, 1), :], (16, layers))
            rows_in[first + a, wide_cols:wide_cols + 16] = jnp.where(
                which == 0, low, jnp.where(which == 1, high, 0.0)).astype(BF16)
        for a in range(0, count, 2):
            pair = jnp.concatenate([rows_in[first + a], rows_in[first + a + 1]], axis=1)
            got = jnp.dot(shift[...], pair, preferred_element_type=F32)
            for b in range(2):
                samp[first + a + b] = got[:cols, b * layers:(b + 1) * layers]
                gy[(first + a + b) % 16] = got[cols:, b * layers:(b + 1) * layers]

    @pl.when(p == 0)
    def _():
        fetch(0, 2, steps).start()

        @pl.loop(0, steps)
        def _(k):
            fetch(8 * k + 2, 8, k).start()
        rimcol[...] = extra[...].astype(F32)
        y = lax.broadcasted_iota(jnp.int32, (cols, shift.shape[1]), 0)
        k = lax.broadcasted_iota(jnp.int32, (cols, shift.shape[1]), 1)
        place = jnp.where(k < wide_cols, k - side,
                          jnp.where(k == wide_cols, -side - 1,
                                    jnp.where(k == wide_cols + 1, cols + side, 1 << 20)))
        gap = place - y - map_ref[1]
        shift[:cols] = jnp.where(gap == 0, 1.0, 0.0).astype(BF16)
        shift[cols:] = (jnp.where(gap == 1, 1.0, 0.0) - jnp.where(gap == -1, 1.0, 0.0)).astype(BF16)
        nel = by_node.shape[0]
        nodes[0:nel, 0:nel] = by_node[...]
        nodes[nel, 0:nel] = edges[0]
        top = lax.broadcasted_iota(jnp.int32, (QPAD - nel, 128), 0) == 0
        for i in range(nel + 1):
            row = edges[1, i:i + 1] if i < nel else edges[2, 0:1]
            nodes[i, nel:QPAD] = jnp.where(top, jnp.broadcast_to(row, (QPAD - nel, 128)), 0.0)
        flat = nodes[...].reshape(-1, 128)
        high = flat.astype(BF16).astype(F32)
        both = jnp.concatenate([high, flat - high], axis=1).astype(BF16)
        level = jnp.dot(both, up[...], preferred_element_type=F32)
        for i in range(ndz.shape[0]):
            part = level[i * QPAD:(i + 1) * QPAD]
            head = part.astype(BF16).astype(F32)
            ndz[i] = jnp.concatenate([head, part - head], axis=0).astype(BF16)
        strain_pull(ns, nodes, pull)
        gacc[...] = jnp.zeros_like(gacc)
        dacc[...] = jnp.zeros_like(dacc)
        fetch(0, 2, steps).wait()
        sample(0, 2)

    base = pl.multiple_of(8 * p, 8)
    fetch(base + 2, 8, p).wait()
    sample(base + 2, 8)
    gz[...] = jnp.dot(samp[pl.ds(base + 1, 8)].reshape(8 * cols, layers).astype(BF16), dz[...],
                      preferred_element_type=F32)
    level = ndz[pl.ds(p, 2)].reshape(4 * QPAD, comps * layers)
    moved[...] = jnp.dot(inter[...], level, preferred_element_type=F32)

    chunk = 32

    @pl.loop(0, cols // chunk)
    def _(j):
        at = pl.multiple_of(j * chunk, chunk)
        span = pl.ds(at, chunk)
        run = [None] * comps
        tot = [None] * comps
        for k in range(8):
            line = pl.ds(k * cols + at, chunk)
            here = samp[base + 1 + k, span, :]
            g = [samp[base + 2 + k, span, :] - samp[base + k, span, :],
                 gy[(base + 1 + k) % 16, span, :],
                 gz[line, :]]
            r = ref_tile[k, span, :].astype(F32) - here
            for c in range(3):
                r = r - g[c] * moved[line, c * layers:(c + 1) * layers]
            res[k, span, :] = r.astype(BF16)
            for c in range(3):
                f = g[c] * r
                run[c] = f if k == 0 else run[c] + f
                tot[c] = run[c] if k == 0 else tot[c] + run[c]
                sq[line, c * layers:(c + 1) * layers] = (g[c] * g[c]).astype(BF16)
        for c in range(3):
            low = (tot[c] - 0.5 * run[c]) * 0.125
            for a, value in enumerate((low, run[c] - low)):
                head, tail = split(value)
                sums[a, span, c * layers:(c + 1) * layers] = head
                sums[a, pl.ds(cols + at, chunk), c * layers:(c + 1) * layers] = tail

    for a in range(2):
        gacc[p + a] = gacc[p + a] + jnp.dot(proj[...], sums[a], preferred_element_type=F32)
    got = jnp.dot(diag[...], sq[...], preferred_element_type=F32)
    for a in range(2):
        dacc[p + a] = dacc[p + a] + (got[a * QPAD:(a + 1) * QPAD] + got[(2 + a) * QPAD:(3 + a) * QPAD])

    @pl.when(p == steps - 1)
    def _():
        for k, (acc, table) in enumerate(((gacc, down), (dacc, down2))):
            head, tail = split(acc[...].reshape(-1, comps * layers))
            got = (jnp.dot(head, table[...], preferred_element_type=F32)
                   + jnp.dot(tail, table[...], preferred_element_type=F32)).reshape(pull.shape)
            out[k] = got + pull[...] if k == 0 else got


def tile_terms(reference_tile, ext, extra, by_node, edges, offsets, ns):
    rows, cols, layers = reference_tile.shape
    comps = 3
    npx = by_node.shape[0] + 1
    rim = rows // 4 + 1
    tabs = tables(rows, cols, layers, comps)
    steps = rows // 8
    whole = lambda a: pl.BlockSpec(a.shape, lambda p, m: (0,) * a.ndim, pipeline_mode=pl.Buffered(1))
    slab = pl.BlockSpec((8, cols, layers), lambda p, m: (p, 0, 0))
    out_nodes = jax.ShapeDtypeStruct((2, npx, QPAD, 128), F32)
    depth = cols + 2 * (rim - 1) + 16
    grid_spec = pltpu.PrefetchScalarGridSpec(
        num_scalar_prefetch=1,
        grid=(steps,),
        in_specs=[slab, pl.BlockSpec(memory_space=pl.ANY), whole(extra), whole(by_node), whole(edges)]
        + [whole(t) for t in tabs],
        out_specs=[slab, whole(out_nodes)],
        scratch_shapes=[
            pltpu.VMEM((rows + 2, depth, layers), BF16),
            pltpu.VMEM((2 * cols, depth), BF16),
            pltpu.VMEM((rows + 2, cols, layers), F32),
            pltpu.VMEM((npx, 2 * QPAD, comps * layers), BF16),
            pltpu.VMEM((8 * cols, comps * layers), F32),
            pltpu.VMEM((16, cols, layers), F32),
            pltpu.VMEM((8 * cols, layers), F32),
            pltpu.VMEM((2, 2 * cols, comps * layers), BF16),
            pltpu.VMEM((8 * cols, comps * layers), BF16),
            pltpu.VMEM((npx, QPAD, comps * layers), F32),
            pltpu.VMEM((npx, QPAD, comps * layers), F32),
            pltpu.VMEM((npx, QPAD, 128), F32),
            pltpu.VMEM((npx, QPAD, 128), F32),
            pltpu.VMEM(extra.shape, F32),
            pltpu.SemaphoreType.DMA((steps + 1,)),
        ],
    )
    return pl.pallas_call(
        functools.partial(tile_kernel, rim, ns),
        grid_spec=grid_spec,
        out_shape=[jax.ShapeDtypeStruct(reference_tile.shape, BF16), out_nodes],
        compiler_params=pltpu.CompilerParams(
            dimension_semantics=("arbitrary",), vmem_limit_bytes=62 << 20),
        name="tile",
    )(offsets, reference_tile, ext, extra, by_node, edges, *tabs)


def node_kernel(nw, nn, terms, by_node, out, column, from_w, from_n, from_c, send, recv):
    nel = by_node.shape[0]
    w = lax.axis_index("wide")
    n = lax.axis_index("narrow")
    lo_w, hi_w, lo_n, hi_n = w > 0, w < nw - 1, n > 0, n < nn - 1
    up_w, dn_w = (w + 1, n), (w - 1, n)
    up_n, dn_n = (w, n + 1), (w, n - 1)
    for ref in (from_w, from_n, from_c):
        ref[...] = jnp.zeros_like(ref)
    barrier = pltpu.get_barrier_semaphore()
    for there, device in ((lo_w, dn_w), (hi_w, up_w), (lo_n, dn_n), (hi_n, up_n)):
        @pl.when(there)
        def _(device=device):
            pl.semaphore_signal(barrier, inc=1, device_id=device, device_id_type=MESH)
    for k in range(2):
        for p in range(nel):
            column[k, p:p + 1] = terms[k, p, nel:nel + 1]
    pl.semaphore_wait(barrier, as_int(lo_w) + as_int(hi_w) + as_int(lo_n) + as_int(hi_n))

    def remote(k, src, dst, device):
        return pltpu.make_async_remote_copy(
            src_ref=src, dst_ref=dst, send_sem=send.at[k], recv_sem=recv.at[k],
            device_id=device, device_id_type=MESH)

    wide_copy = remote(0, terms.at[:, nel], from_w, up_w)
    narrow_copy = remote(1, column, from_n, up_n)
    corner_copy = remote(2, from_w.at[:, nel:QPAD], from_c, up_n)

    @pl.when(hi_w)
    def _():
        wide_copy.start()

    @pl.when(hi_n)
    def _():
        narrow_copy.start()

    @pl.when(lo_w)
    def _():
        wide_copy.wait_recv()

    @pl.when(lo_w & hi_n)
    def _():
        corner_copy.start()

    @pl.when(lo_n)
    def _():
        narrow_copy.wait_recv()

    @pl.when(lo_w & lo_n)
    def _():
        corner_copy.wait_recv()

    top = lax.broadcasted_iota(jnp.int32, (nel, 128), 0) == 0
    for p in range(nel):
        sums = []
        for k in range(2):
            value = terms[k, p, 0:nel]
            side = from_n[k, p:p + 1]
            if p == 0:
                value = value + from_w[k, 0:nel]
                side = side + from_c[k, 0:1]
            sums.append(value + jnp.where(top, jnp.broadcast_to(side, (nel, 128)), 0.0))
        out[p] = by_node[p] - sums[0] / (sums[1] + STIFFNESS)

    @pl.when(hi_w)
    def _():
        wide_copy.wait_send()

    @pl.when(hi_n)
    def _():
        narrow_copy.wait_send()

    @pl.when(lo_w & hi_n)
    def _():
        corner_copy.wait_send()


def node_update(terms, by_node, nw, nn):
    nel = by_node.shape[0]
    near = pl.BlockSpec(memory_space=pltpu.VMEM)
    return pl.pallas_call(
        functools.partial(node_kernel, nw, nn),
        out_shape=jax.ShapeDtypeStruct(by_node.shape, F32),
        in_specs=[near, near],
        out_specs=near,
        scratch_shapes=[
            pltpu.VMEM((2, nel, 128), F32),
            pltpu.VMEM((2, QPAD, 128), F32),
            pltpu.VMEM((2, nel, 128), F32),
            pltpu.VMEM((2, QPAD - nel, 128), F32),
            pltpu.SemaphoreType.DMA((3,)),
            pltpu.SemaphoreType.DMA((3,)),
        ],
        compiler_params=pltpu.CompilerParams(collective_id=1, has_side_effects=True),
        name="nodes",
    )(terms, by_node)


def per_device(nw, nn, reference_image, deformed_image, displacement, tile_map):
    comps, ns, nex, ney = displacement.shape
    by_node = displacement.transpose(2, 3, 0, 1).reshape(nex, ney, comps * ns)
    by_node = jnp.pad(by_node, ((0, 0), (0, 0), (0, 128 - comps * ns)))
    ext, extra, edges = exchange(deformed_image, by_node, nw, nn)
    residual, terms = tile_terms(
        reference_image, ext, extra, by_node, edges, tile_map.reshape(2), ns)
    moved = node_update(terms, by_node, nw, nn)
    updated = moved[:, :, :comps * ns].reshape(nex, ney, comps, ns).transpose(2, 3, 0, 1)
    return (updated, residual)


def solution(mesh):
    placed = (
        P("wide", "narrow", None),
        P("wide", "narrow", None),
        P(None, None, "wide", "narrow"),
        P("wide", "narrow", None),
    )
    return jax.shard_map(
        functools.partial(per_device, mesh.shape["wide"], mesh.shape["narrow"]),
        mesh=mesh,
        in_specs=placed,
        out_specs=(P(None, None, "wide", "narrow"), P("wide", "narrow", None)),
        check_vma=False,
    )
```

```python
import functools

import jax
import jax.numpy as jnp
import numpy as np
from jax import lax
from jax.experimental import pallas as pl
from jax.experimental.pallas import tpu as pltpu
from jax.sharding import PartitionSpec as P

MU_SHEAR = 1.0
LAMBDA_BULK = 2.0
REG_WEIGHT = 256.0
STIFFNESS = 16.0
MESH = pl.DeviceIdType.MESH
F32 = jnp.float32
BF16 = jnp.bfloat16
SIDE = 48
QPAD = 24


def as_int(flag):
    return flag.astype(jnp.int32)


def fill_nodes(nodes, by_node, edges):
    nel = by_node.shape[0]
    nodes[0:nel, 0:nel] = by_node[...]
    nodes[nel, 0:nel] = edges[0]
    top = lax.broadcasted_iota(jnp.int32, (QPAD - nel, 128), 0) == 0
    for i in range(nel + 1):
        row = edges[1, i:i + 1] if i < nel else edges[2, 0:1]
        nodes[i, nel:QPAD] = jnp.where(top, jnp.broadcast_to(row, (QPAD - nel, 128)), 0.0)


def strain_pull(ns, nodes, pull):
    npx = nodes.shape[0]
    nel = npx - 1
    lane = lax.broadcasted_iota(jnp.int32, (nel, 128), 1)
    move = lambda a, by: pltpu.roll(a, by % 128, 1)
    pull[...] = jnp.zeros_like(pull)

    @pl.loop(0, nel)
    def _(p):
        a00, a01 = nodes[p, 0:nel], nodes[p, 1:nel + 1]
        a10, a11 = nodes[p + 1, 0:nel], nodes[p + 1, 1:nel + 1]
        dx = (a10 - a00) + (a11 - a01)
        dy = (a01 - a00) + (a11 - a10)
        every = (a00 + a01) + (a10 + a11)
        slopes = (dx + move(dx, -1), dy + move(dy, -1), move(every, -1) - every)
        f = [[0.03125 * (move(h, -ns * i) if i else h) + (1.0 if i == j else 0.0)
              for j, h in enumerate(slopes)] for i in range(3)]
        cof = [[f[(i + 1) % 3][(j + 1) % 3] * f[(i + 2) % 3][(j + 2) % 3]
                - f[(i + 1) % 3][(j + 2) % 3] * f[(i + 2) % 3][(j + 1) % 3]
                for j in range(3)] for i in range(3)]
        ratio = f[0][0] * cof[0][0] + f[0][1] * cof[0][1] + f[0][2] * cof[0][2]
        factor = (LAMBDA_BULK * jnp.log(ratio) - MU_SHEAR) / ratio
        back = []
        for j in range(3):
            parts = [jnp.where(lane < ns - 1, MU_SHEAR * f[i][j] + factor * cof[i][j], 0.0) for i in range(3)]
            back.append((parts[0] + move(parts[1], ns) + move(parts[2], 2 * ns)) * (0.03125 * REG_WEIGHT))
        gx = back[0] + move(back[0], 1)
        gy = back[1] + move(back[1], 1)
        gz = move(back[2], 1) - back[2]
        for dp, dq in ((0, 0), (0, 1), (1, 0), (1, 1)):
            add = (gx if dp else -gx) + (gy if dq else -gy) + gz
            pull[p + dp, dq:dq + nel] = pull[p + dp, dq:dq + nel] + add


def halo_kernel(nw, nn, rim, ns, own, extra_in, edge_x, edge_y, by_node, out, extra, nodes, pull,
                edges, ext, zeros, send, recv, zsem, lsem):
    rows, cols, _ = own.shape
    side = rim - 1
    w = lax.axis_index("wide")
    n = lax.axis_index("narrow")
    lo_w, hi_w, lo_n, hi_n = w > 0, w < nw - 1, n > 0, n < nn - 1
    up_w, dn_w = (w + 1, n), (w - 1, n)
    up_n, dn_n = (w, n + 1), (w, n - 1)
    mid = slice(side, side + cols)
    ylo = slice(0, side)
    yhi = slice(side + cols, 2 * side + cols)
    total = rows + 2 * rim
    emid = slice(SIDE, SIDE + rows)
    local = pltpu.make_async_copy(own, ext.at[rim:rim + rows, mid], lsem.at[0])
    local.start()
    edges[...] = jnp.zeros_like(edges)
    extra[...] = jnp.zeros_like(extra)
    barrier = pltpu.get_barrier_semaphore()
    for there, device in ((lo_w, dn_w), (hi_w, up_w), (lo_n, dn_n), (hi_n, up_n)):
        @pl.when(there)
        def _(device=device):
            pl.semaphore_signal(barrier, inc=1, device_id=device, device_id_type=MESH)
    zeros[...] = jnp.zeros_like(zeros)
    jobs = []

    def fill(cond, dst):
        src = zeros.at[tuple(slice(0, d) for d in dst.shape)]
        jobs.append((cond, pltpu.make_async_copy(src, dst, zsem.at[len(jobs)])))

    for cond, span in ((jnp.logical_not(lo_n), ylo), (jnp.logical_not(hi_n), yhi)):
        fill(cond, ext.at[:, span])
    for cond, band in ((jnp.logical_not(lo_w), slice(0, rim)), (jnp.logical_not(hi_w), slice(rim + rows, total))):
        fill(cond, ext.at[band, mid])
        fill(cond & lo_n, ext.at[band, ylo])
        fill(cond & hi_n, ext.at[band, yhi])
    for cond, job in jobs:
        @pl.when(cond)
        def _(job=job):
            job.start()
    pl.semaphore_wait(barrier, as_int(lo_w) + as_int(hi_w) + as_int(lo_n) + as_int(hi_n))

    def remote(k, src, dst, device):
        return pltpu.make_async_remote_copy(
            src_ref=src, dst_ref=dst, send_sem=send.at[k], recv_sem=recv.at[k],
            device_id=device, device_id_type=MESH)

    first = [
        (lo_w, hi_w, remote(0, edge_x, edges.at[0], dn_w)),
        (lo_n, hi_n, remote(1, edge_y, edges.at[1], dn_n)),
        (hi_n, lo_n, remote(2, extra_in.at[0], extra.at[0, emid], up_n)),
        (lo_n, hi_n, remote(3, extra_in.at[1], extra.at[1, emid], dn_n)),
    ]
    full = (slice(0, rim), slice(rows - rim, rows), slice(rim, rows - rim))
    for j, part in enumerate(full):
        if j == 2:
            first.append((hi_w, lo_w, remote(10, ext.at[rows:rows + rim, mid], ext.at[0:rim, mid], up_w)))
            first.append((lo_w, hi_w, remote(11, ext.at[rim:2 * rim, mid], ext.at[rows + rim:total, mid], dn_w)))
        there = slice(part.start + rim, part.stop + rim)
        first.append((hi_n, lo_n, remote(4 + 2 * j, ext.at[there, cols:cols + side], ext.at[there, ylo], up_n)))
        first.append((lo_n, hi_n, remote(5 + 2 * j, ext.at[there, side:2 * side], ext.at[there, yhi], dn_n)))
    local.wait()
    saves = []

    def settle(k, span, columns):
        save = pltpu.make_async_copy(ext.at[span, columns], out.at[span, columns], lsem.at[1 + k])
        save.start()
        saves.append(save)

    for goes, _c, copy in first:
        @pl.when(goes)
        def _(copy=copy):
            copy.start()
    settle(0, slice(rim, rim + rows), mid)
    low_rows, high_rows = slice(rim, 2 * rim), slice(rows, rows + rim)
    below, above = slice(0, rim), slice(rim + rows, total)
    elow, ehigh = slice(SIDE, 2 * SIDE), slice(rows, SIDE + rows)
    ebelow, eabove = slice(0, SIDE), slice(SIDE + rows, 2 * SIDE + rows)
    second = {
        0: [(hi_w & lo_n, hi_w & hi_n, remote(12, edges.at[0], edges.at[2], dn_n))],
        2: [(lo_n & lo_w, lo_n & hi_w, remote(13, extra.at[0, elow], extra.at[0, eabove], dn_w)),
            (lo_n & hi_w, lo_n & lo_w, remote(14, extra.at[0, ehigh], extra.at[0, ebelow], up_w))],
        3: [(hi_n & lo_w, hi_n & hi_w, remote(15, extra.at[1, elow], extra.at[1, eabove], dn_w)),
            (hi_n & hi_w, hi_n & lo_w, remote(16, extra.at[1, ehigh], extra.at[1, ebelow], up_w))],
        4: [(lo_n & lo_w, lo_n & hi_w, remote(17, ext.at[low_rows, ylo], ext.at[above, ylo], dn_w))],
        5: [(hi_n & lo_w, hi_n & hi_w, remote(18, ext.at[low_rows, yhi], ext.at[above, yhi], dn_w))],
        6: [(lo_n & hi_w, lo_n & lo_w, remote(19, ext.at[high_rows, ylo], ext.at[below, ylo], up_w))],
        7: [(hi_n & hi_w, hi_n & lo_w, remote(20, ext.at[high_rows, yhi], ext.at[below, yhi], up_w))],
    }
    later = []
    for k, (_g, comes, copy) in enumerate(first):
        @pl.when(comes)
        def _(copy=copy):
            copy.wait_recv()
        for entry in second.get(k, ()):
            later.append(entry)
            @pl.when(entry[0])
            def _(entry=entry):
                entry[2].start()
        if k == 3:
            @pl.when(later[0][1])
            def _():
                later[0][2].wait_recv()
            fill_nodes(nodes, by_node, edges)
            strain_pull(ns, nodes, pull)
    for _g, comes, copy in later[1:]:
        @pl.when(comes)
        def _(copy=copy):
            copy.wait_recv()
    for cond, job in jobs:
        @pl.when(cond)
        def _(job=job):
            job.wait()
    settle(1, below, mid)
    settle(2, above, mid)
    settle(3, slice(0, total), ylo)
    settle(4, slice(0, total), yhi)
    for goes, _c, copy in first + later:
        @pl.when(goes)
        def _(copy=copy):
            copy.wait_send()
    for save in saves:
        save.wait()


def exchange(deformed, by_node, ns, nw, nn):
    rows, cols, layers = deformed.shape
    rim = rows // 4 + 1
    shape = (rows + 2 * rim, cols + 2 * (rim - 1), layers)
    extra_in = jnp.stack([deformed[:, cols - rim], deformed[:, rim - 1]])
    anywhere = pl.BlockSpec(memory_space=pl.ANY)
    near = pl.BlockSpec(memory_space=pltpu.VMEM)
    nodes = jax.ShapeDtypeStruct((by_node.shape[0] + 1, QPAD, 128), F32)
    return pl.pallas_call(
        functools.partial(halo_kernel, nw, nn, rim, ns),
        out_shape=[jax.ShapeDtypeStruct(shape, BF16),
                   jax.ShapeDtypeStruct((2, rows + 2 * SIDE, layers), BF16),
                   nodes, nodes],
        in_specs=[anywhere, near, near, near, near],
        out_specs=[anywhere, near, near, near],
        scratch_shapes=[
            pltpu.VMEM((3,) + by_node.shape[1:], F32),
            pltpu.VMEM(shape, BF16),
            pltpu.VMEM((shape[0], cols, layers), BF16),
            pltpu.SemaphoreType.DMA((21,)),
            pltpu.SemaphoreType.DMA((21,)),
            pltpu.SemaphoreType.DMA((8,)),
            pltpu.SemaphoreType.DMA((6,)),
        ],
        compiler_params=pltpu.CompilerParams(
            collective_id=0, has_side_effects=True, vmem_limit_bytes=62 << 20),
        name="halo",
    )(deformed, extra_in, by_node[0], by_node[:, 0], by_node)


def tables(rows, cols, layers, comps):
    def one(voxels):
        t = np.zeros((voxels, voxels // 8 + 1))
        for i in range(voxels):
            f = (i % 8 + 0.5) / 8.0
            t[i, i // 8] += 1.0 - f
            t[i, i // 8 + 1] += f
        return t
    ty, tz = one(cols), one(layers)
    nq, ns = ty.shape[1], tz.shape[1]
    typ = np.zeros((cols, QPAD))
    typ[:, :nq] = ty
    frac = (np.arange(8) + 0.5) / 8.0
    wx = np.stack([1.0 - frac, frac], 1)
    inter = 0.5 * np.einsum("ka,yq->kyaq", wx, typ)
    inter = np.concatenate([inter[:, :, 0], inter[:, :, 0], inter[:, :, 1], inter[:, :, 1]], -1)
    inter = inter.reshape(8 * cols, 4 * QPAD)
    proj = np.concatenate([typ.T, typ.T], 1)
    diag = np.einsum("ka,yq->aqky", wx * wx, typ * typ).reshape(2 * QPAD, 8 * cols)
    dhi = diag.astype(BF16).astype(np.float64)
    diag = np.concatenate([dhi, diag - dhi], 0)
    lanes = comps * layers
    up = np.zeros((2 * 128, lanes))
    down = np.zeros((lanes, 128))
    down2 = np.zeros((lanes, 128))
    for c in range(comps):
        for h in range(2):
            up[h * 128 + c * ns:h * 128 + (c + 1) * ns, c * layers:(c + 1) * layers] = tz.T
        down[c * layers:(c + 1) * layers, c * ns:(c + 1) * ns] = -0.5 * tz
        down2[c * layers:(c + 1) * layers, c * ns:(c + 1) * ns] = 0.25 * tz * tz
    dz = np.zeros((layers, layers))
    for z in range(layers):
        if z + 1 < layers:
            dz[z + 1, z] = 1.0
        if z > 0:
            dz[z - 1, z] = -1.0
    as_bf16 = lambda a: jnp.asarray(a.astype(BF16))
    return [as_bf16(a) for a in (inter, proj, diag, up, down, down2, dz)]


def split(value):
    high = value.astype(BF16)
    return high, (value - high.astype(F32)).astype(BF16)


def tile_kernel(rim, map_ref, ref_tile, ext, extra, nodes, pull,
                inter, proj, diag, up, down, down2, dz,
                res, out,
                rows_in, shift, samp, ndz, moved, gy, gz, sums, sq, gacc, dacc, rimcol, sem):
    p = pl.program_id(0)
    steps = pl.num_programs(0)
    cols, layers = samp.shape[1], samp.shape[2]
    comps = ndz.shape[2] // layers
    side = rim - 1
    wide_cols = cols + 2 * side
    start = map_ref[0] + side

    def fetch(first, count, k):
        return pltpu.make_async_copy(
            ext.at[pl.ds(start + first, count)],
            rows_in.at[pl.ds(first, count), 0:wide_cols], sem.at[k])

    def sample(first, count):
        for a in range(count):
            at = map_ref[0] + (SIDE - 1) + first + a
            which = lax.broadcasted_iota(jnp.int32, (16, layers), 0)
            low = jnp.broadcast_to(rimcol[0, pl.ds(at, 1), :], (16, layers))
            high = jnp.broadcast_to(rimcol[1, pl.ds(at, 1), :], (16, layers))
            rows_in[first + a, wide_cols:wide_cols + 16] = jnp.where(
                which == 0, low, jnp.where(which == 1, high, 0.0)).astype(BF16)
        for a in range(0, count, 2):
            pair = jnp.concatenate([rows_in[first + a], rows_in[first + a + 1]], axis=1)
            got = jnp.dot(shift[...], pair, preferred_element_type=F32)
            for b in range(2):
                samp[first + a + b] = got[:cols, b * layers:(b + 1) * layers]
                gy[(first + a + b) % 16] = got[cols:, b * layers:(b + 1) * layers]

    @pl.when(p == 0)
    def _():
        fetch(0, 2, steps).start()

        @pl.loop(0, steps)
        def _(k):
            fetch(8 * k + 2, 8, k).start()
        rimcol[...] = extra[...].astype(F32)
        y = lax.broadcasted_iota(jnp.int32, (cols, shift.shape[1]), 0)
        k = lax.broadcasted_iota(jnp.int32, (cols, shift.shape[1]), 1)
        place = jnp.where(k < wide_cols, k - side,
                          jnp.where(k == wide_cols, -side - 1,
                                    jnp.where(k == wide_cols + 1, cols + side, 1 << 20)))
        gap = place - y - map_ref[1]
        shift[:cols] = jnp.where(gap == 0, 1.0, 0.0).astype(BF16)
        shift[cols:] = (jnp.where(gap == 1, 1.0, 0.0) - jnp.where(gap == -1, 1.0, 0.0)).astype(BF16)
        flat = nodes[...].reshape(-1, 128)
        high = flat.astype(BF16).astype(F32)
        both = jnp.concatenate([high, flat - high], axis=1).astype(BF16)
        level = jnp.dot(both, up[...], preferred_element_type=F32)
        for i in range(ndz.shape[0]):
            part = level[i * QPAD:(i + 1) * QPAD]
            head = part.astype(BF16).astype(F32)
            ndz[i] = jnp.concatenate([head, part - head], axis=0).astype(BF16)
        gacc[...] = jnp.zeros_like(gacc)
        dacc[...] = jnp.zeros_like(dacc)
        fetch(0, 2, steps).wait()
        sample(0, 2)

    base = pl.multiple_of(8 * p, 8)
    fetch(base + 2, 8, p).wait()
    sample(base + 2, 8)
    gz[...] = jnp.dot(samp[pl.ds(base + 1, 8)].reshape(8 * cols, layers).astype(BF16), dz[...],
                      preferred_element_type=F32)
    level = ndz[pl.ds(p, 2)].reshape(4 * QPAD, comps * layers)
    moved[...] = jnp.dot(inter[...], level, preferred_element_type=F32)

    chunk = 32

    @pl.loop(0, cols // chunk)
    def _(j):
        at = pl.multiple_of(j * chunk, chunk)
        span = pl.ds(at, chunk)
        run = [None] * comps
        tot = [None] * comps
        for k in range(8):
            line = pl.ds(k * cols + at, chunk)
            here = samp[base + 1 + k, span, :]
            g = [samp[base + 2 + k, span, :] - samp[base + k, span, :],
                 gy[(base + 1 + k) % 16, span, :],
                 gz[line, :]]
            r = ref_tile[k, span, :].astype(F32) - here
            for c in range(3):
                r = r - g[c] * moved[line, c * layers:(c + 1) * layers]
            res[k, span, :] = r.astype(BF16)
            for c in range(3):
                f = g[c] * r
                run[c] = f if k == 0 else run[c] + f
                tot[c] = run[c] if k == 0 else tot[c] + run[c]
                sq[line, c * layers:(c + 1) * layers] = (g[c] * g[c]).astype(BF16)
        for c in range(3):
            low = (tot[c] - 0.5 * run[c]) * 0.125
            for a, value in enumerate((low, run[c] - low)):
                head, tail = split(value)
                sums[a, span, c * layers:(c + 1) * layers] = head
                sums[a, pl.ds(cols + at, chunk), c * layers:(c + 1) * layers] = tail

    for a in range(2):
        gacc[p + a] = gacc[p + a] + jnp.dot(proj[...], sums[a], preferred_element_type=F32)
    got = jnp.dot(diag[...], sq[...], preferred_element_type=F32)
    for a in range(2):
        dacc[p + a] = dacc[p + a] + (got[a * QPAD:(a + 1) * QPAD] + got[(2 + a) * QPAD:(3 + a) * QPAD])

    @pl.when(p == steps - 1)
    def _():
        for k, (acc, table) in enumerate(((gacc, down), (dacc, down2))):
            head, tail = split(acc[...].reshape(-1, comps * layers))
            got = (jnp.dot(head, table[...], preferred_element_type=F32)
                   + jnp.dot(tail, table[...], preferred_element_type=F32)).reshape(pull.shape)
            out[k] = got + pull[...] if k == 0 else got


def tile_terms(reference_tile, ext, extra, nodes, pull, offsets):
    rows, cols, layers = reference_tile.shape
    comps = 3
    npx = nodes.shape[0]
    rim = rows // 4 + 1
    tabs = tables(rows, cols, layers, comps)
    steps = rows // 8
    whole = lambda a: pl.BlockSpec(a.shape, lambda p, m: (0,) * a.ndim, pipeline_mode=pl.Buffered(1))
    slab = pl.BlockSpec((8, cols, layers), lambda p, m: (p, 0, 0))
    out_nodes = jax.ShapeDtypeStruct((2, npx, QPAD, 128), F32)
    depth = cols + 2 * (rim - 1) + 16
    grid_spec = pltpu.PrefetchScalarGridSpec(
        num_scalar_prefetch=1,
        grid=(steps,),
        in_specs=[slab, pl.BlockSpec(memory_space=pl.ANY), whole(extra), whole(nodes), whole(pull)]
        + [whole(t) for t in tabs],
        out_specs=[slab, whole(out_nodes)],
        scratch_shapes=[
            pltpu.VMEM((rows + 2, depth, layers), BF16),
            pltpu.VMEM((2 * cols, depth), BF16),
            pltpu.VMEM((rows + 2, cols, layers), F32),
            pltpu.VMEM((npx, 2 * QPAD, comps * layers), BF16),
            pltpu.VMEM((8 * cols, comps * layers), F32),
            pltpu.VMEM((16, cols, layers), F32),
            pltpu.VMEM((8 * cols, layers), F32),
            pltpu.VMEM((2, 2 * cols, comps * layers), BF16),
            pltpu.VMEM((8 * cols, comps * layers), BF16),
            pltpu.VMEM((npx, QPAD, comps * layers), F32),
            pltpu.VMEM((npx, QPAD, comps * layers), F32),
            pltpu.VMEM(extra.shape, F32),
            pltpu.SemaphoreType.DMA((steps + 1,)),
        ],
    )
    return pl.pallas_call(
        functools.partial(tile_kernel, rim),
        grid_spec=grid_spec,
        out_shape=[jax.ShapeDtypeStruct(reference_tile.shape, BF16), out_nodes],
        compiler_params=pltpu.CompilerParams(
            dimension_semantics=("arbitrary",), vmem_limit_bytes=62 << 20),
        name="tile",
    )(offsets, reference_tile, ext, extra, nodes, pull, *tabs)


def node_kernel(nw, nn, terms, by_node, out, column, from_w, from_n, from_c, send, recv):
    nel = by_node.shape[0]
    w = lax.axis_index("wide")
    n = lax.axis_index("narrow")
    lo_w, hi_w, lo_n, hi_n = w > 0, w < nw - 1, n > 0, n < nn - 1
    up_w, dn_w = (w + 1, n), (w - 1, n)
    up_n, dn_n = (w, n + 1), (w, n - 1)
    for ref in (from_w, from_n, from_c):
        ref[...] = jnp.zeros_like(ref)
    barrier = pltpu.get_barrier_semaphore()
    for there, device in ((lo_w, dn_w), (hi_w, up_w), (lo_n, dn_n), (hi_n, up_n)):
        @pl.when(there)
        def _(device=device):
            pl.semaphore_signal(barrier, inc=1, device_id=device, device_id_type=MESH)
    for k in range(2):
        for p in range(nel):
            column[k, p:p + 1] = terms[k, p, nel:nel + 1]
    pl.semaphore_wait(barrier, as_int(lo_w) + as_int(hi_w) + as_int(lo_n) + as_int(hi_n))

    def remote(k, src, dst, device):
        return pltpu.make_async_remote_copy(
            src_ref=src, dst_ref=dst, send_sem=send.at[k], recv_sem=recv.at[k],
            device_id=device, device_id_type=MESH)

    wide_copy = remote(0, terms.at[:, nel], from_w, up_w)
    narrow_copy = remote(1, column, from_n, up_n)
    corner_copy = remote(2, from_w.at[:, nel:QPAD], from_c, up_n)

    @pl.when(hi_w)
    def _():
        wide_copy.start()

    @pl.when(hi_n)
    def _():
        narrow_copy.start()

    @pl.when(lo_w)
    def _():
        wide_copy.wait_recv()

    @pl.when(lo_w & hi_n)
    def _():
        corner_copy.start()

    @pl.when(lo_n)
    def _():
        narrow_copy.wait_recv()

    @pl.when(lo_w & lo_n)
    def _():
        corner_copy.wait_recv()

    top = lax.broadcasted_iota(jnp.int32, (nel, 128), 0) == 0
    for p in range(nel):
        sums = []
        for k in range(2):
            value = terms[k, p, 0:nel]
            side = from_n[k, p:p + 1]
            if p == 0:
                value = value + from_w[k, 0:nel]
                side = side + from_c[k, 0:1]
            sums.append(value + jnp.where(top, jnp.broadcast_to(side, (nel, 128)), 0.0))
        out[p] = by_node[p] - sums[0] / (sums[1] + STIFFNESS)

    @pl.when(hi_w)
    def _():
        wide_copy.wait_send()

    @pl.when(hi_n)
    def _():
        narrow_copy.wait_send()

    @pl.when(lo_w & hi_n)
    def _():
        corner_copy.wait_send()


def node_update(terms, by_node, nw, nn):
    nel = by_node.shape[0]
    near = pl.BlockSpec(memory_space=pltpu.VMEM)
    return pl.pallas_call(
        functools.partial(node_kernel, nw, nn),
        out_shape=jax.ShapeDtypeStruct(by_node.shape, F32),
        in_specs=[near, near],
        out_specs=near,
        scratch_shapes=[
            pltpu.VMEM((2, nel, 128), F32),
            pltpu.VMEM((2, QPAD, 128), F32),
            pltpu.VMEM((2, nel, 128), F32),
            pltpu.VMEM((2, QPAD - nel, 128), F32),
            pltpu.SemaphoreType.DMA((3,)),
            pltpu.SemaphoreType.DMA((3,)),
        ],
        compiler_params=pltpu.CompilerParams(collective_id=1, has_side_effects=True),
        name="nodes",
    )(terms, by_node)


def per_device(nw, nn, reference_image, deformed_image, displacement, tile_map):
    comps, ns, nex, ney = displacement.shape
    by_node = displacement.transpose(2, 3, 0, 1).reshape(nex, ney, comps * ns)
    by_node = jnp.pad(by_node, ((0, 0), (0, 0), (0, 128 - comps * ns)))
    ext, extra, nodes, pull = exchange(deformed_image, by_node, ns, nw, nn)
    residual, terms = tile_terms(
        reference_image, ext, extra, nodes, pull, tile_map.reshape(2))
    moved = node_update(terms, by_node, nw, nn)
    updated = moved[:, :, :comps * ns].reshape(nex, ney, comps, ns).transpose(2, 3, 0, 1)
    return (updated, residual)


def solution(mesh):
    placed = (
        P("wide", "narrow", None),
        P("wide", "narrow", None),
        P(None, None, "wide", "narrow"),
        P("wide", "narrow", None),
    )
    return jax.shard_map(
        functools.partial(per_device, mesh.shape["wide"], mesh.shape["narrow"]),
        mesh=mesh,
        in_specs=placed,
        out_specs=(P(None, None, "wide", "narrow"), P("wide", "narrow", None)),
        check_vma=False,
    )
```
